32 devices in a mesh: dp: 2 (over core), ctx: 16 (over z, y, x).
Axes of the slice: x: 2, y: 2, z: 4, core: 2. Of those that a mesh axis runs over, the one named last changes fastest.
Arguments:
- layer_in: bfloat16 [2, 4096, 768], P('dp', 'ctx'), may hold values from -6 to 6
- out_grad: bfloat16 [2, 4096, 768], P('dp', 'ctx'), may hold values from -6 to 6
- first_gain: bfloat16 [768], P('dp'), may hold values from 0.099609375 to 1.8984375
- query_weight: bfloat16 [768, 768], P('dp'), may hold values from -0.21875 to 0.21875
- key_weight: bfloat16 [768, 768], P('dp'), may hold values from -0.21875 to 0.21875
- value_weight: bfloat16 [768, 768], P('dp'), may hold values from -0.21875 to 0.21875
- output_weight: bfloat16 [768, 768], P('dp'), may hold values from -6 to 6
- second_gain: bfloat16 [768], P('dp'), may hold values from 0.099609375 to 1.8984375
- gate_weight: bfloat16 [768, 2048], P('dp'), may hold values from -0.21875 to 0.21875
- up_weight: bfloat16 [768, 2048], P('dp'), may hold values from -0.21875 to 0.21875
- down_weight: bfloat16 [2048, 768], P('dp'), may hold values from -0.125 to 0.125
Outputs:
- layer_out: bfloat16 [2, 4096, 768], P('dp', 'ctx')
- in_grad: bfloat16 [2, 4096, 768], P('dp', 'ctx')
- first_gain_grad: float32 [768], P('dp')
- query_grad: float32 [768, 768], P('dp')
- key_grad: float32 [768, 768], P('dp')
- value_grad: float32 [768, 768], P('dp')
- output_grad: float32 [768, 768], P('dp')
- second_gain_grad: float32 [768], P('dp')
- gate_grad: float32 [768, 2048], P('dp')
- up_grad: float32 [768, 2048], P('dp')
- down_grad: float32 [2048, 768], P('dp')
The draws below stay inside these ranges and needn't reach their ends.
All inputs are finite; a program needn't handle non-finite values.
Results may differ from the reference program's by a relative error of at most 0.02.
Values may be sent and summed in bfloat16 or wider, within the bound.
No kernel may reach another device: no remote copies, remote signals or barrier semaphores. Data moves between devices by JAX's collectives and lax.ppermute only.
A program may use at most 448 MiB of HBM per device.

```python
import jax
import jax.numpy as jnp
from jax import lax

D = 768
HEADS = 12
HEAD_DIM = 64
FF = 2048
LEN = 4096
BATCH = 2


def block_levels(own_key, extent, shards, low, largest):
    level, own = 1.0, jax.random.fold_in(own_key, 6)
    for position, shards_of in shards:
        heights = jnp.exp(jax.random.uniform(jax.random.fold_in(own, position), (shards_of,), jnp.float32, low / len(shards), largest / len(shards)))
        level = level * jnp.repeat(heights, extent[position] // shards_of).reshape([-1 if axis == position else 1 for axis in range(len(extent))])
    return level


def centred(stream_key, extent, width, most, shards=(), held_as=jnp.bfloat16):
    values = jax.random.normal(stream_key, extent, jnp.float32) * width
    if len(shards) > 0:
        values = block_levels(stream_key, extent, shards, -0.22, 0.18) * values
    return jnp.clip(values, min=-most, max=most).astype(held_as)


def setup_inputs(seed: int = 0) -> dict:
    seeds = jax.random.split(jax.random.key(seed), 12)
    layer_in = centred(seeds[0], (BATCH, LEN, D), 1.0, 6.0, ((0, 2), (1, 16)))
    out_grad = centred(seeds[1], (BATCH, LEN, D), 1.0, 6.0, ((0, 2), (1, 16)))
    first_gain = jnp.clip(1.0 + 0.18 * jax.random.normal(seeds[2], (D,), jnp.float32), 0.099609375, 1.8984375).astype(jnp.bfloat16)
    query_weight = centred(seeds[3], (D, D), D ** -0.5, 0.21875, ((0, 2),))
    key_weight = centred(seeds[4], (D, D), D ** -0.5, 0.21875, ((0, 2),))
    value_weight = centred(seeds[5], (D, D), D ** -0.5, 0.21875, ((0, 2),))
    output_weight = centred(seeds[6], (D, D), (max(1, 3 * D // LEN)) ** -0.5, 6.0, ((0, 2),))
    second_gain = jnp.clip(1.0 + 0.18 * jax.random.normal(seeds[7], (D,), jnp.float32), 0.099609375, 1.8984375).astype(jnp.bfloat16)
    gate_weight = centred(seeds[8], (D, FF), D ** -0.5, 0.21875, ((0, 2),))
    up_weight = centred(seeds[9], (D, FF), D ** -0.5, 0.21875, ((0, 2),))
    down_weight = centred(seeds[10], (FF, D), FF ** -0.5, 0.125, ((0, 2),))
    return dict(layer_in=layer_in, out_grad=out_grad, first_gain=first_gain, query_weight=query_weight, key_weight=key_weight, value_weight=value_weight, output_weight=output_weight, second_gain=second_gain, gate_weight=gate_weight, up_weight=up_weight, down_weight=down_weight)


@jax.custom_vjp
def low(v):
    return lax.optimization_barrier(v.astype(jnp.bfloat16)).astype(jnp.float32)

@jax.custom_vjp
def low_back(v):
    return v

def low_keep(v):
    return (low(v), None)

def low_pass(kept, grad):
    return (grad,)

def back_keep(v):
    return (v, None)

def back_low(kept, grad):
    return (low(grad),)
low.defvjp(low_keep, low_pass)
low_back.defvjp(back_keep, back_low)
EPS = 1e-06

def normed(rows, gain):
    return rows * lax.rsqrt(lax.optimization_barrier(jnp.mean(rows * rows, axis=-1, keepdims=True)) + EPS) * gain

def matmul(left, right):
    return jnp.dot(left, right, precision=lax.Precision.HIGHEST)

def layer_seq(params, seq_rows):
    gain_one, w_query, w_key, w_value, w_output, gain_two, w_gate, w_up, w_down = params
    length = seq_rows.shape[0]
    normal_one = low(normed(seq_rows, gain_one))
    query = low_back(low(matmul(normal_one, w_query)))
    keys = low_back(low(matmul(normal_one, w_key)))
    values = low_back(low(matmul(normal_one, w_value)))
    query_h = query.reshape(length, HEADS, HEAD_DIM)
    keys_h = keys.reshape(length, HEADS, HEAD_DIM)
    values_h = values.reshape(length, HEADS, HEAD_DIM)
    scores = low_back(jnp.einsum('qhd,khd->hqk', query_h, keys_h, precision=lax.Precision.HIGHEST) * HEAD_DIM ** (-0.5))
    probs = low(jax.nn.softmax(scores, axis=-1))
    mixed = jnp.einsum('hqk,khd->qhd', probs, values_h, precision=lax.Precision.HIGHEST).reshape(length, HEADS * HEAD_DIM)
    mixed = low_back(low(mixed))
    branch = low_back(matmul(mixed, w_output))
    middle = seq_rows + branch
    normal_two = low(normed(middle, gain_two))
    gate = low_back(matmul(normal_two, w_gate))
    upper = low_back(matmul(normal_two, w_up))
    hidden = low(jax.nn.gelu(gate, approximate=True) * upper)
    return middle + matmul(hidden, w_down)

def reference(layer_in, out_grad, first_gain, query_weight, key_weight, value_weight, output_weight, second_gain, gate_weight, up_weight, down_weight):
    inputs = layer_in.astype(jnp.float32)
    params = tuple((w.astype(jnp.float32) for w in (first_gain, query_weight, key_weight, value_weight, output_weight, second_gain, gate_weight, up_weight, down_weight)))

    def forward(whole, weights):
        return lax.map(jax.checkpoint(lambda seq_rows: layer_seq(weights, seq_rows)), whole)
    result, pull = jax.vjp(forward, inputs, params)
    grad_in, grads = pull(out_grad.astype(jnp.float32))
    return (result.astype(jnp.bfloat16), grad_in.astype(jnp.bfloat16), grads[0], grads[1], grads[2], grads[3], grads[4], grads[5], grads[6], grads[7], grads[8])
```

```python
import functools
import math

import jax
import jax.numpy as jnp
from jax import lax
from jax.experimental import pallas as pl
from jax.experimental.pallas import tpu as pltpu
from jax.sharding import PartitionSpec as P

HEADS = 12
HEAD_DIM = 64
EPS = 1e-06
LOG2E = 1.4426950408889634
SCALE = HEAD_DIM ** (-0.5)
AXES = ("dp", "ctx")
F32 = jnp.float32
BF16 = jnp.bfloat16


def dotg(a, b, ca, cb):
    return lax.dot_general(a, b, (((ca,), (cb,)), ((), ())), preferred_element_type=F32)


def attend_kernel(heads, key_block, q_ref, *refs):
    sources = refs[:-3]
    o_ref, low_ref, lse_ref = refs[-3:]
    tokens = q_ref.shape[1]
    width = heads * HEAD_DIM
    for h in range(heads):
        hs = slice(h * HEAD_DIM, (h + 1) * HEAD_DIM)
        vs = slice(width + h * HEAD_DIM, width + (h + 1) * HEAD_DIM)
        query = q_ref[hs, :] * BF16(SCALE)
        top = jnp.full((1, tokens), -jnp.inf, F32)
        total = jnp.zeros((1, tokens), F32)
        acc = jnp.zeros((HEAD_DIM, tokens), F32)
        for source in sources:
            for at in range(0, source.shape[1], key_block):
                ks = slice(at, at + key_block)
                scores = dotg(source[hs, ks], query, 0, 0) * LOG2E
                new_top = jnp.maximum(top, jnp.max(scores, axis=0, keepdims=True))
                decay = jnp.exp2(top - new_top)
                probs = jnp.exp2(scores - new_top)
                total = total * decay + jnp.sum(probs, axis=0, keepdims=True)
                acc = acc * decay + jnp.dot(
                    source[vs, ks], probs.astype(BF16), preferred_element_type=F32
                )
                top = new_top
        out = acc / total
        o_ref[hs, :] = out
        low_ref[hs, :] = out.astype(BF16)
        lse_ref[h : h + 1, :] = top + jnp.log2(total)


def attend(query, sources, key_block=1024):
    width, tokens = query.shape
    heads = width // HEAD_DIM
    return pl.pallas_call(
        functools.partial(attend_kernel, heads, key_block),
        out_shape=(
            jax.ShapeDtypeStruct((width, tokens), F32),
            jax.ShapeDtypeStruct((width, tokens), BF16),
            jax.ShapeDtypeStruct((heads, tokens), F32),
        ),
        compiler_params=pltpu.CompilerParams(vmem_limit_bytes=60 << 20),
        name="attend",
    )(query, *sources)


def attend_back_kernel(heads, key_block, q_ref, do_ref, o_ref, lse_ref, *refs):
    n = (len(refs) - 1) // 2
    sources, dq_ref, outs = refs[:n], refs[n], refs[n + 1 :]
    width = heads * HEAD_DIM
    for h in range(heads):
        hs = slice(h * HEAD_DIM, (h + 1) * HEAD_DIM)
        vs = slice(width + h * HEAD_DIM, width + (h + 1) * HEAD_DIM)
        query = q_ref[hs, :] * BF16(SCALE)
        grad = do_ref[hs, :]
        lse = lse_ref[h : h + 1, :]
        delta = jnp.sum(grad.astype(F32) * o_ref[hs, :], axis=0, keepdims=True)
        dq = jnp.zeros(query.shape, F32)
        for source, out in zip(sources, outs):
            for at in range(0, source.shape[1], key_block):
                ks = slice(at, at + key_block)
                keys, values = source[hs, ks], source[vs, ks]
                probs = jnp.exp2(dotg(keys, query, 0, 0) * LOG2E - lse)
                gap = dotg(values, grad, 0, 0) - delta
                low = probs.astype(BF16)
                ds = (probs * gap).astype(BF16)
                out[vs, ks] = dotg(grad, low, 1, 1).astype(BF16)
                out[hs, ks] = dotg(query, ds, 1, 1).astype(BF16)
                dq = dq + jnp.dot(keys, ds, preferred_element_type=F32)
        dq_ref[hs, :] = (dq * SCALE).astype(BF16)


def attend_back(query, grad, out, lse, sources, key_block=256):
    heads = query.shape[0] // HEAD_DIM
    outs = pl.pallas_call(
        functools.partial(attend_back_kernel, heads, key_block),
        out_shape=(jax.ShapeDtypeStruct(query.shape, BF16),)
        + tuple(jax.ShapeDtypeStruct(s.shape, BF16) for s in sources),
        compiler_params=pltpu.CompilerParams(vmem_limit_bytes=60 << 20),
        name="attend_back",
    )(query, grad, out, lse, *sources)
    return outs[0], list(outs[1:])


class Plan:
    def __init__(self, dp, ctx):
        self.dp, self.ctx = dp, ctx
        self.groups = math.gcd(HEADS, ctx)
        self.rest = ctx // self.groups
        self.bits = self.rest.bit_length() - 1
        assert 1 << self.bits == self.rest and self.groups & (self.groups - 1) == 0

    def bit(self, parity, step):
        return step if parity == 0 else self.bits - 1 - step

    def rest_perm(self, step):
        return [
            (d * self.ctx + c, d * self.ctx + (c ^ (1 << self.bit(d % 2, step))))
            for d in range(self.dp)
            for c in range(self.ctx)
        ]

    def group_perm(self, s):
        return [(c, c ^ (s * self.rest)) for c in range(self.ctx)]

    def group(self):
        return lax.axis_index("ctx") // self.rest

    def my_bit(self, step):
        c = lax.axis_index("ctx")
        even = (c >> self.bit(0, step)) & 1
        odd = (c >> self.bit(1, step)) & 1
        return jnp.where(lax.axis_index("dp") % 2 == 0, even, odd)

    def over_rest(self, value, step):
        return lax.ppermute(value, AXES, self.rest_perm(step))

    def over_group(self, value, s):
        return value if s == 0 else lax.ppermute(value, "ctx", self.group_perm(s))

    def gather_rest(self, value):
        blocks = [value]
        for step in range(self.bits):
            blocks = blocks + [self.over_rest(b, step) for b in blocks]
        return blocks

    def scatter_rest(self, blocks):
        for step in reversed(range(self.bits)):
            half = len(blocks) // 2
            came = [self.over_rest(b, step) for b in blocks[half:]]
            blocks = [add_low(a, b) for a, b in zip(blocks[:half], came)]
        return blocks[0]

    def to_heads(self, value):
        size = value.shape[0] // self.groups
        return [
            self.over_group(
                lax.dynamic_slice_in_dim(value, (self.group() ^ s) * size, size, 0), s
            )
            for s in range(self.groups)
        ]

    def to_tokens(self, pieces):
        came = [self.over_group(p, s) for s, p in enumerate(pieces)]
        return self.natural(came)

    def natural(self, pieces):
        g = self.group()
        step = 1
        while step < self.groups:
            odd = (g & step) != 0
            pieces = [
                jnp.where(odd, pieces[i ^ step], pieces[i]) for i in range(self.groups)
            ]
            step *= 2
        return jnp.concatenate(pieces, axis=0)

    def sum_ctx(self, value):
        for step in range(self.bits):
            half = value.shape[0] // 2
            b = self.my_bit(step)
            kept = lax.dynamic_slice_in_dim(value, b * half, half, 0)
            gone = lax.dynamic_slice_in_dim(value, (1 - b) * half, half, 0)
            value = add_low(kept, self.over_rest(gone, step))
        pieces = self.to_heads(value)
        value = functools.reduce(jnp.add, [p.astype(F32) for p in pieces]).astype(BF16)
        value = self.natural(
            [self.over_group(value, s) for s in range(self.groups)]
        )
        for step in reversed(range(self.bits)):
            b = self.my_bit(step)
            came = self.over_rest(value, step)
            value = jnp.where(
                b == 0,
                jnp.concatenate([value, came], axis=0),
                jnp.concatenate([came, value], axis=0),
            )
        return value.astype(F32)

    def sum_small(self, value):
        for step in range(self.bits):
            value = value + self.over_rest(value, step)
        return functools.reduce(
            jnp.add, [self.over_group(value, s) for s in range(self.groups)]
        )


def add_low(a, b):
    return (a.astype(F32) + b.astype(F32)).astype(BF16)


class Pair:
    def __init__(self, dp):
        self.dp = dp
        self.me = lax.axis_index("dp")

    def swap(self, value):
        return lax.ppermute(value, "dp", [(0, 1), (1, 0)])

    def gather(self, weight):
        if self.dp == 2:
            return [weight, self.swap(weight)]
        return [lax.all_gather(weight, "dp", axis=0, tiled=True)]

    def part(self, value, i, axis):
        if self.dp != 2:
            return value
        half = value.shape[axis] // 2
        at = jnp.where(self.me == i, 0, half)
        return lax.dynamic_slice_in_dim(value, at, half, axis)

    def join(self, parts, axis):
        if len(parts) == 1:
            return parts[0]
        return jnp.where(
            self.me == 0,
            jnp.concatenate(parts, axis),
            jnp.concatenate(parts[::-1], axis),
        )

    def times(self, value, axis, weight, contract):
        return functools.reduce(
            jnp.add,
            [
                contract(self.part(value, i, axis), w)
                for i, w in enumerate(weight)
            ],
        )

    def grad(self, left, row_axis, right, right_axis):
        token_axis = 1 - row_axis
        if self.dp != 2:
            return lax.psum_scatter(
                dotg(left, right, token_axis, right_axis).astype(BF16),
                "dp",
                scatter_dimension=0,
                tiled=True,
            )
        own, other = self.part(left, 0, row_axis), self.part(left, 1, row_axis)
        lefts = jnp.concatenate([own, self.swap(other)], token_axis)
        rights = jnp.concatenate([right, self.swap(right)], right_axis)
        return dotg(lefts, rights, token_axis, right_axis).astype(BF16)

    def gain(self, part):
        if self.dp != 2:
            return lax.psum_scatter(part, "dp", scatter_dimension=0, tiled=True)
        return self.part(part, 0, 0) + self.swap(self.part(part, 1, 0))


def scaled(rows):
    return lax.rsqrt(jnp.mean(rows * rows, axis=-1, keepdims=True) + EPS)


def gated(gate, upper):
    return jax.nn.gelu(gate, approximate=True) * upper


def norm_back(rows, r, gain, grad):
    lead = gain * grad
    back = r * (lead - rows * (r * r) * jnp.mean(lead * rows, axis=-1, keepdims=True))
    return back, jnp.sum(grad * rows * r, axis=0)


def on_device(
    dp,
    ctx,
    layer_in,
    out_grad,
    first_gain,
    query_weight,
    key_weight,
    value_weight,
    output_weight,
    second_gain,
    gate_weight,
    up_weight,
    down_weight,
):
    plan, pair = Plan(dp, ctx), Pair(dp)
    _, local, width = layer_in.shape
    group_width = width // plan.groups

    gain_one = pair.join(pair.gather(first_gain), 0).astype(F32)
    w_query, w_key, w_value = (
        pair.gather(w) for w in (query_weight, key_weight, value_weight)
    )
    x = layer_in.reshape(local, width).astype(F32)
    r1 = scaled(x)
    h1 = (x * r1 * gain_one).astype(BF16)

    def project(w):
        return pair.times(h1, 1, w, lambda a, b: dotg(b, a, 0, 1)).astype(BF16)

    keys, values, query = project(w_key), project(w_value), project(w_query)
    kv_pieces = [
        jnp.concatenate(p, axis=0) for p in zip(plan.to_heads(keys), plan.to_heads(values))
    ]
    kv = jnp.concatenate(kv_pieces, axis=1)
    q = jnp.concatenate(plan.to_heads(query), axis=1)
    sources = plan.gather_rest(kv)
    o_wide, o_low, lse = attend(q, sources)

    def by_token(value):
        return [value[:, i * local : (i + 1) * local] for i in range(plan.groups)]

    mixed = plan.to_tokens(by_token(o_low))

    w_output = pair.gather(output_weight)
    gain_two = pair.join(pair.gather(second_gain), 0).astype(F32)
    w_gate, w_up, w_down = (pair.gather(w) for w in (gate_weight, up_weight, down_weight))
    y1 = x + pair.times(mixed, 0, w_output, lambda a, b: dotg(a, b, 0, 0))
    r2 = scaled(y1)
    h2 = (y1 * r2 * gain_two).astype(BF16)
    gate = pair.times(h2, 1, w_gate, lambda a, b: dotg(a, b, 1, 0))
    upper = pair.times(h2, 1, w_up, lambda a, b: dotg(a, b, 1, 0))
    hidden = gated(gate, upper).astype(BF16)
    result = y1 + pair.times(hidden, 1, w_down, lambda a, b: dotg(a, b, 1, 0))
    layer_out = result.astype(BF16).reshape(layer_in.shape)

    dy = out_grad.reshape(local, width)
    down_term = pair.grad(hidden, 1, dy, 0)
    grad_hidden = pair.join([dotg(dy, w, 1, 1) for w in w_down], 1)
    _, gate_back = jax.vjp(gated, gate, upper)
    d_gate, d_up = gate_back(grad_hidden)
    d_gate, d_up = d_gate.astype(BF16), d_up.astype(BF16)
    gate_term = pair.grad(h2, 1, d_gate, 0)
    up_term = pair.grad(h2, 1, d_up, 0)
    dh2 = pair.join(
        [dotg(d_gate, a, 1, 1) + dotg(d_up, b, 1, 1) for a, b in zip(w_gate, w_up)], 1
    )
    back_two, gain_two_part = norm_back(y1, r2, gain_two, dh2)
    dy1 = back_two + dy.astype(F32)
    da = dy1.astype(BF16)
    output_term = pair.grad(mixed, 0, da, 0)
    d_mixed = pair.join([dotg(w, da, 1, 1) for w in w_output], 0).astype(BF16)

    do = jnp.concatenate(plan.to_heads(d_mixed), axis=1)
    dq, dkv = attend_back(q, do, o_wide, lse, sources)
    dkv = plan.scatter_rest(dkv)
    d_query = plan.to_tokens(by_token(dq))
    d_key = plan.to_tokens(by_token(dkv[:group_width]))
    d_value = plan.to_tokens(by_token(dkv[group_width:]))
    query_term = pair.grad(h1, 1, d_query, 1)
    key_term = pair.grad(h1, 1, d_key, 1)
    value_term = pair.grad(h1, 1, d_value, 1)
    dh1 = pair.join(
        [
            dotg(d_query, a, 0, 1) + dotg(d_key, b, 0, 1) + dotg(d_value, c, 0, 1)
            for a, b, c in zip(w_query, w_key, w_value)
        ],
        1,
    )
    back_one, gain_one_part = norm_back(x, r1, gain_one, dh1)
    in_grad = (back_one + dy1).astype(BF16).reshape(layer_in.shape)

    gains = plan.sum_small(
        jnp.stack([pair.gain(gain_one_part), pair.gain(gain_two_part)])
    )
    return (
        layer_out,
        in_grad,
        gains[0],
        plan.sum_ctx(query_term),
        plan.sum_ctx(key_term),
        plan.sum_ctx(value_term),
        plan.sum_ctx(output_term),
        gains[1],
        plan.sum_ctx(gate_term),
        plan.sum_ctx(up_term),
        plan.sum_ctx(down_term),
    )


def solution(mesh):
    tokens, matrix, vector = P("dp", "ctx", None), P("dp", None), P("dp")
    weights = (vector, matrix, matrix, matrix, matrix, vector, matrix, matrix, matrix)
    return jax.shard_map(
        functools.partial(on_device, mesh.shape["dp"], mesh.shape["ctx"]),
        mesh=mesh,
        in_specs=(tokens, tokens) + weights,
        out_specs=(tokens, tokens) + weights,
        check_vma=False,
    )
```

```python
import functools
import math

import jax
import jax.numpy as jnp
from jax import lax
from jax.experimental import pallas as pl
from jax.experimental.pallas import tpu as pltpu
from jax.sharding import PartitionSpec as P

HEADS = 12
HEAD_DIM = 64
EPS = 1e-06
LOG2E = 1.4426950408889634
SCALE = HEAD_DIM ** (-0.5)
AXES = ("dp", "ctx")
F32 = jnp.float32
BF16 = jnp.bfloat16


def dotg(a, b, ca, cb):
    return lax.dot_general(a, b, (((ca,), (cb,)), ((), ())), preferred_element_type=F32)


def attend_kernel(key_block, q_ref, *refs):
    sources = refs[:-3]
    o_ref, low_ref, lse_ref = refs[-3:]
    tokens = q_ref.shape[1]
    query = q_ref[...] * BF16(SCALE)
    top = jnp.full((1, tokens), -jnp.inf, F32)
    total = jnp.zeros((1, tokens), F32)
    acc = jnp.zeros((HEAD_DIM, tokens), F32)
    for source in sources:
        for at in range(0, source.shape[1], key_block):
            ks = slice(at, at + key_block)
            scores = dotg(source[:HEAD_DIM, ks], query, 0, 0) * LOG2E
            new_top = jnp.maximum(top, jnp.max(scores, axis=0, keepdims=True))
            decay = jnp.exp2(top - new_top)
            probs = jnp.exp2(scores - new_top)
            total = total * decay + jnp.sum(probs, axis=0, keepdims=True)
            acc = acc * decay + jnp.dot(
                source[HEAD_DIM:, ks], probs.astype(BF16), preferred_element_type=F32
            )
            top = new_top
    out = acc / total
    o_ref[...] = out
    low_ref[...] = out.astype(BF16)
    lse_ref[...] = top + jnp.log2(total)


def cost(flops, nbytes):
    return pl.CostEstimate(flops=flops * 10, transcendentals=0, bytes_accessed=nbytes)


def attend(head, query, sources, key_block=1024):
    tokens = query.shape[1]
    keys = sum(s.shape[1] for s in sources)
    whole = lambda s: pl.BlockSpec(s.shape, lambda i: (0, 0))
    flat = lambda rows: pl.BlockSpec((rows, tokens), lambda i: (0, 0))
    return pl.pallas_call(
        functools.partial(attend_kernel, key_block),
        grid=(1,),
        in_specs=[pl.BlockSpec((HEAD_DIM, tokens), lambda i: (head, 0))]
        + [whole(s) for s in sources],
        out_specs=(flat(HEAD_DIM), flat(HEAD_DIM), flat(1)),
        out_shape=(
            jax.ShapeDtypeStruct((HEAD_DIM, tokens), F32),
            jax.ShapeDtypeStruct((HEAD_DIM, tokens), BF16),
            jax.ShapeDtypeStruct((1, tokens), F32),
        ),
        compiler_params=pltpu.CompilerParams(vmem_limit_bytes=60 << 20),
        cost_estimate=cost(4 * 4 * HEAD_DIM * tokens * keys, 0),
        name="attend",
    )(query, *sources)


def attend_back_kernel(key_block, n, q_ref, do_ref, o_ref, lse_ref, *refs):
    sources, dq_ref, outs = refs[:n], refs[n], refs[n + 1 :]
    query = q_ref[...] * BF16(SCALE)
    grad = do_ref[...]
    lse = lse_ref[...]
    delta = jnp.sum(grad.astype(F32) * o_ref[...], axis=0, keepdims=True)
    dq = jnp.zeros(query.shape, F32)
    tokens = sources[0].shape[1]
    for i, source in enumerate(sources):
        out, base = outs[i * len(outs) // n], i % (n // len(outs)) * tokens
        for at in range(0, tokens, key_block):
            ks = slice(at, at + key_block)
            to = slice(base + at, base + at + key_block)
            keys, values = source[:HEAD_DIM, ks], source[HEAD_DIM:, ks]
            probs = jnp.exp2(dotg(keys, query, 0, 0) * LOG2E - lse)
            gap = dotg(values, grad, 0, 0) - delta
            low = probs.astype(BF16)
            ds = (probs * gap).astype(BF16)
            out[HEAD_DIM:, to] = dotg(grad, low, 1, 1).astype(BF16)
            out[:HEAD_DIM, to] = dotg(query, ds, 1, 1).astype(BF16)
            dq = dq + jnp.dot(keys, ds, preferred_element_type=F32)
    dq_ref[...] = (dq * SCALE).astype(BF16)


def attend_back(head, query, grad, out, lse, sources, key_block=256):
    tokens = query.shape[1]
    n = len(sources)
    parts = min(n, 2)
    keys = sum(s.shape[1] for s in sources)
    whole = lambda s: pl.BlockSpec(s.shape, lambda i: (0, 0))
    mine = lambda: pl.BlockSpec((HEAD_DIM, tokens), lambda i: (head, 0))
    shapes = (jax.ShapeDtypeStruct((HEAD_DIM, tokens), BF16),) + tuple(
        jax.ShapeDtypeStruct((2 * HEAD_DIM, keys // parts), BF16) for _ in range(parts)
    )
    outs = pl.pallas_call(
        functools.partial(attend_back_kernel, key_block, n),
        grid=(1,),
        in_specs=[mine(), mine(), whole(out), whole(lse)] + [whole(s) for s in sources],
        out_specs=tuple(whole(s) for s in shapes),
        out_shape=shapes,
        compiler_params=pltpu.CompilerParams(vmem_limit_bytes=60 << 20),
        cost_estimate=cost(4 * 10 * HEAD_DIM * tokens * keys, 0),
        name="attend_back",
    )(query, grad, out, lse, *sources)
    return outs[0], list(outs[1:])


def copies(pair, parts, full, sems):
    half = parts[0].shape[0]
    made = []
    for i, part in enumerate(parts):
        at = 0 if len(parts) == 1 else pl.multiple_of((pair ^ i) * half, half)
        made.append(pltpu.make_async_copy(part, full.at[pl.ds(at, half), :], sems.at[i]))
    return made


def middle_kernel(groups, parts, chunk, place_ref, x_ref, dy_ref, gain_ref, *refs):
    pieces = refs[:groups]
    given = refs[groups : groups + 4 * parts]
    rest = refs[groups + 4 * parts :]
    (out_ref, dy1_ref, mixed_ref, h2_ref, hidden_ref, dgate_ref, dup_ref, da_ref) = rest[:8]
    back_pieces = rest[8 : 8 + groups]
    wo, wg, wu, wd, do_ref, sems = rest[8 + groups :]
    pair, group = place_ref[0], place_ref[1]
    made = [
        copies(pair, given[j * parts : (j + 1) * parts], full, sems.at[j])
        for j, full in enumerate((wo, wg, wu, wd))
    ]
    for cs in made:
        for c in cs:
            c.start()
    rows = pieces[0].shape[0]
    spot = [pl.ds(pl.multiple_of((group ^ s) * rows, rows), rows) for s in range(groups)]
    for s in range(groups):
        mixed_ref[spot[s], :] = pieces[s][...]
    for c in made[0]:
        c.wait()
    dy = dy_ref[...]
    gain = gain_ref[...].astype(F32)
    y1 = x_ref[...].astype(F32) + dotg(mixed_ref[...], wo[...], 0, 0)
    r2 = lax.rsqrt(jnp.mean(y1 * y1, axis=-1, keepdims=True) + EPS)
    h2 = (y1 * r2 * gain).astype(BF16)
    h2_ref[...] = h2
    for cs in made[1:]:
        for c in cs:
            c.wait()
    result = y1
    dh2 = jnp.zeros(y1.shape, F32)
    root, cubic = math.sqrt(2 / math.pi), 0.044715
    for at in range(0, wg.shape[1], chunk):
        cs = slice(at, at + chunk)
        u = jnp.dot(h2, wg[:, cs], preferred_element_type=F32)
        upper = jnp.dot(h2, wu[:, cs], preferred_element_type=F32)
        square = u * u
        t = jnp.tanh(root * (u + cubic * (u * square)))
        share = 0.5 * (1.0 + t)
        bent = u * share
        slope = share + (0.5 * root) * u * (1.0 - t * t) * (1.0 + (3 * cubic) * square)
        hidden = (bent * upper).astype(BF16)
        hidden_ref[:, cs] = hidden
        result = result + jnp.dot(hidden, wd[cs, :], preferred_element_type=F32)
        dhidden = dotg(dy, wd[cs, :], 1, 1)
        dgate = (dhidden * upper * slope).astype(BF16)
        dup = (dhidden * bent).astype(BF16)
        dgate_ref[:, cs] = dgate
        dup_ref[:, cs] = dup
        dh2 = dh2 + dotg(dgate, wg[:, cs], 1, 1) + dotg(dup, wu[:, cs], 1, 1)
    out_ref[...] = result.astype(BF16)
    lead = gain * dh2
    mean = jnp.mean(lead * y1, axis=-1, keepdims=True)
    dy1 = dy.astype(F32) + r2 * (lead - y1 * (r2 * r2) * mean)
    dy1_ref[...] = dy1
    da = dy1.astype(BF16)
    da_ref[...] = da
    do_ref[...] = dotg(wo[...], da, 1, 1).astype(BF16)
    for s in range(groups):
        back_pieces[s][...] = do_ref[spot[s], :]


def middle(place, x, dy, gain, pieces, weights, ff):
    tokens, width = x.shape
    groups, parts = len(pieces), len(weights[0])
    vmem = pl.BlockSpec(memory_space=pltpu.VMEM)
    some = lambda shape, dtype: jax.ShapeDtypeStruct(shape, dtype)
    wide = some((tokens, ff), BF16)
    flat = some((tokens, width), BF16)
    outs = pl.pallas_call(
        functools.partial(middle_kernel, groups, parts, 512),
        in_specs=[pl.BlockSpec(memory_space=pltpu.SMEM)]
        + [vmem] * (3 + groups)
        + [pl.BlockSpec(memory_space=pl.ANY)] * (4 * parts),
        out_specs=(vmem,) * (8 + groups),
        out_shape=(
            flat,
            some((tokens, width), F32),
            some((width, tokens), BF16),
            flat,
            wide,
            wide,
            wide,
            flat,
        )
        + tuple(some(p.shape, BF16) for p in pieces),
        scratch_shapes=[
            pltpu.VMEM((width, width), BF16),
            pltpu.VMEM((width, ff), BF16),
            pltpu.VMEM((width, ff), BF16),
            pltpu.VMEM((ff, width), BF16),
            pltpu.VMEM((width, tokens), BF16),
            pltpu.SemaphoreType.DMA((4, parts)),
        ],
        compiler_params=pltpu.CompilerParams(vmem_limit_bytes=60 << 20),
        cost_estimate=cost(4 * tokens * width * (width + 3 * ff), 6 * width * ff),
        name="middle",
    )(place, x, dy, gain.reshape(1, width), *pieces, *[p for w in weights for p in w])
    return outs[:8], list(outs[8:])


def grads_kernel(parts, axes, place_ref, *refs):
    n = len(axes)
    lefts, rights, outs = refs[:n], refs[n : 2 * n], refs[2 * n :]
    for i, out in enumerate(outs):
        base = 0
        for left, right, axis in zip(lefts, rights, axes):
            rows = left.shape[axis] // parts
            at = pl.multiple_of((place_ref[0] ^ i) * rows, rows) if parts > 1 else 0
            part = left[:, pl.ds(at, rows)] if axis == 1 else left[pl.ds(at, rows), :]
            value = dotg(part, right[...], 1 - axis, 0)
            out[:, base : base + right.shape[1]] = value.astype(BF16)
            base += right.shape[1]


def weight_grads(place, dp, terms):
    parts = 2 if dp == 2 else 1
    lefts, axes, rights = zip(*terms)
    rows = lefts[0].shape[axes[0]] // parts
    columns = sum(r.shape[1] for r in rights)
    vmem = pl.BlockSpec(memory_space=pltpu.VMEM)
    return pl.pallas_call(
        functools.partial(grads_kernel, parts, axes),
        in_specs=[pl.BlockSpec(memory_space=pltpu.SMEM)] + [vmem] * (2 * len(terms)),
        out_specs=(vmem,) * parts,
        out_shape=(jax.ShapeDtypeStruct((rows, columns), BF16),) * parts,
        compiler_params=pltpu.CompilerParams(vmem_limit_bytes=60 << 20),
        cost_estimate=cost(2 * parts * rows * columns * rights[0].shape[0], 0),
        name="weight_grads",
    )(place, *lefts, *rights)


def head_grads_kernel(heads, devices, parts, place_ref, *refs):
    outs = refs[-parts:]
    queries, pairs = refs[:heads], refs[heads : 2 * heads]
    rows = refs[2 * heads : -parts]
    d = jnp.concatenate(
        [q[...] for q in queries]
        + [p[:HEAD_DIM, :] for p in pairs]
        + [p[HEAD_DIM:, :] for p in pairs],
        axis=0,
    )
    width = rows[0].shape[1] // parts
    for i, out in enumerate(outs):
        at = pl.multiple_of((place_ref[0] ^ i) * width, width) if parts > 1 else 0
        left = jnp.concatenate([r[:, pl.ds(at, width)] for r in rows], axis=0)
        out[...] = jnp.dot(d, left, preferred_element_type=F32).T.astype(BF16)


def head_grads(place, dp, queries, pairs, rows):
    heads, parts = len(queries), 2 if dp == 2 else 1
    width, columns = rows[0].shape[1], 3 * HEAD_DIM * heads
    vmem = pl.BlockSpec(memory_space=pltpu.VMEM)
    return pl.pallas_call(
        functools.partial(head_grads_kernel, heads, dp, parts),
        in_specs=[pl.BlockSpec(memory_space=pltpu.SMEM)] + [vmem] * (2 * heads + len(rows)),
        out_specs=(vmem,) * parts,
        out_shape=(jax.ShapeDtypeStruct((width // parts, columns), BF16),) * parts,
        compiler_params=pltpu.CompilerParams(vmem_limit_bytes=60 << 20),
        cost_estimate=cost(2 * queries[0].shape[1] * width * columns, 0),
        name="head_grads",
    )(place, *queries, *pairs, *rows)


def unstacked(value, base, rows, cols):
    n = cols // LANES
    part = value[base : base + rows * n].reshape(n, rows, LANES)
    return part.transpose(1, 0, 2).reshape(rows, cols).astype(F32)


class Plan:
    def __init__(self, dp, ctx):
        self.dp, self.ctx = dp, ctx
        self.groups = math.gcd(HEADS, ctx)
        self.rest = ctx // self.groups
        self.bits = self.rest.bit_length() - 1
        self.group_bits = self.groups.bit_length() - 1
        assert 1 << self.bits == self.rest and self.groups & (self.groups - 1) == 0

    def bit(self, parity, step):
        return step if parity == 0 else self.bits - 1 - step

    def rest_perm(self, step):
        return [
            (d * self.ctx + c, d * self.ctx + (c ^ (1 << self.bit(d % 2, step))))
            for d in range(self.dp)
            for c in range(self.ctx)
        ]

    def group_perm(self, s):
        return [(c, c ^ (s * self.rest)) for c in range(self.ctx)]

    def group(self):
        return lax.axis_index("ctx") // self.rest

    def my_bit(self, step):
        c = lax.axis_index("ctx")
        even = (c >> self.bit(0, step)) & 1
        odd = (c >> self.bit(1, step)) & 1
        return jnp.where(lax.axis_index("dp") % 2 == 0, even, odd)

    def over_rest(self, value, step):
        return lax.ppermute(value, AXES, self.rest_perm(step))

    def over_group(self, value, s):
        return value if s == 0 else lax.ppermute(value, "ctx", self.group_perm(s))

    def gather_rest(self, value):
        blocks = [value]
        for step in range(self.bits):
            came = yield [
                (b, lambda v, step=step: self.over_rest(v, step)) for b in blocks
            ]
            blocks = blocks + came
        return blocks

    def natural(self, pieces, axis=0):
        g = self.group()
        step = 1
        while step < self.groups:
            odd = (g & step) != 0
            pieces = [
                jnp.where(odd, pieces[i ^ step], pieces[i]) for i in range(self.groups)
            ]
            step *= 2
        return jnp.concatenate(pieces, axis=axis)

    def hop(self, step):
        if step < self.bits:
            return lambda v: self.over_rest(v, step)
        return lambda v: self.over_group(v, 1 << (step - self.bits))

    def place_bit(self, step):
        if step < self.bits:
            return self.my_bit(step)
        return (self.group() >> (step - self.bits)) & 1

    def halves(self, value, step):
        half = value.shape[0] // 2
        b = self.place_bit(step)
        return (
            lax.dynamic_slice_in_dim(value, b * half, half, 0),
            lax.dynamic_slice_in_dim(value, (1 - b) * half, half, 0),
        )

    def group_pieces(self, value):
        size = value.shape[0] // self.groups
        return [
            lax.dynamic_slice_in_dim(value, (self.group() ^ s) * size, size, 0)
            for s in range(self.groups)
        ]

    def to_rest(self, value, step):
        return [(value, lambda v: self.over_rest(v, step))]

    def to_groups(self, pieces):
        return [
            (p, lambda v, s=s: self.over_group(v, s)) for s, p in enumerate(pieces) if s
        ]

    def exchange(self, pieces):
        came = yield self.to_groups(pieces)
        return [pieces[0]] + came

    def send_group(self, value, s):
        came = yield [(value, lambda v: self.over_group(v, s))]
        return came[0]

    def scatter_rest(self, parts):
        for step in reversed(range(self.bits)):
            if step < self.bits - 1:
                half = parts.shape[1] // 2
                parts = parts[:, :half], parts[:, half:]
            came = yield self.to_rest(parts[1], step)
            parts = add_low(parts[0], came[0])
        return parts if self.bits else parts[0]

    def reduce_rows(self, value, steps):
        for step in range(steps):
            kept, gone = self.halves(value, step)
            came = yield [(gone, self.hop(step))]
            value = add_low(kept, came[0])
        return value

    def expand_rows(self, value, steps):
        for step in reversed(range(steps)):
            came = yield [(value, self.hop(step))]
            value = jnp.where(
                self.place_bit(step) == 0,
                jnp.concatenate([value, came[0]], axis=0),
                jnp.concatenate([came[0], value], axis=0),
            )
        return value

    def sum_rows(self, pair, stacks):
        value = yield from pair.combine(stacks)
        value = yield from self.reduce_rows(value, self.bits + self.group_bits)
        return (yield from self.expand_rows(value, self.bits + self.group_bits))

    def sum_heads(self, pair, stacks, columns):
        value = yield from pair.combine(stacks)
        value = yield from self.reduce_rows(value, self.bits)
        rows, groups = value.shape[0], [value]
        for step in range(self.group_bits):
            came = yield [(jnp.concatenate(groups, axis=0), self.hop(self.bits + step))]
            groups = groups + [
                came[0][i * rows : (i + 1) * rows] for i in range(len(groups))
            ]
        value = jnp.concatenate(
            [
                self.natural([p[:, at : at + columns] for p in groups], 1)
                for at in range(0, value.shape[1], columns)
            ],
            axis=1,
        )
        return (yield from self.expand_rows(value, self.bits))


def add_low(a, b):
    return (a.astype(F32) + b.astype(F32)).astype(BF16)


class Chain:
    def __init__(self, name, stages):
        self.name, self.stages, self.came, self.result = name, stages, None, None
        self.stage = 0

    def send(self, moves, values):
        self.stage += 1
        with jax.named_scope(f"{self.name}_{self.stage}"):
            self.came = [move(v) for v, (_, move) in zip(values, moves)]

    def next_moves(self):
        if self.result is not None:
            return []
        try:
            return self.stages.send(self.came)
        except StopIteration as end:
            self.came, self.result = None, end.value
            return []


class Order:
    def __init__(self, token):
        self.token = token

    def __call__(self, land, launch, values=()):
        moves = [c.next_moves() for c in launch]
        waiting = [c for c in land if c not in launch and c.came is not None]
        ended = [c for c in launch if c.result is not None]
        self.token, values, held, done, sent = lax.optimization_barrier(
            (
                self.token,
                values,
                [c.came for c in waiting],
                [c.result for c in ended],
                [[v for v, _ in m] for m in moves],
            )
        )
        for c, came in zip(waiting, held):
            c.came = came
        for c, result in zip(ended, done):
            c.result = result
        for c, m, vs in zip(launch, moves, sent):
            if m:
                c.send(m, vs)
        return values


def finish(*chains):
    while any(c.result is None for c in chains):
        for c in chains:
            m = c.next_moves()
            if m:
                c.send(m, [v for v, _ in m])
    return [c.result for c in chains]


def add_low(a, b):
    return (a.astype(F32) + b.astype(F32)).astype(BF16)


class Pair:
    def __init__(self, dp):
        self.dp = dp
        self.me = lax.axis_index("dp")

    def swap(self, value):
        return lax.ppermute(value, "dp", [(0, 1), (1, 0)])

    def gather(self, weight):
        if self.dp != 2:
            return [lax.all_gather(weight, "dp", axis=0, tiled=True)]
        came = yield [(weight, self.swap)]
        return [weight] + came

    def part(self, value, i, axis):
        if self.dp != 2:
            return value
        half = value.shape[axis] // 2
        at = jnp.where(self.me == i, 0, half)
        return lax.dynamic_slice_in_dim(value, at, half, axis)

    def join(self, parts, axis):
        if len(parts) == 1:
            return parts[0]
        return jnp.where(
            self.me == 0,
            jnp.concatenate(parts, axis),
            jnp.concatenate(parts[::-1], axis),
        )

    def times(self, value, axis, weight, contract):
        return functools.reduce(
            jnp.add,
            [
                contract(self.part(value, i, axis), w)
                for i, w in enumerate(weight)
            ],
        )

    def combine(self, stacks):
        if self.dp == 2:
            came = yield [(stacks[1], self.swap)]
            return add_low(stacks[0], came[0])
        return lax.psum_scatter(stacks[0], "dp", scatter_dimension=0, tiled=True)


def scaled(rows):
    return lax.rsqrt(jnp.mean(rows * rows, axis=-1, keepdims=True) + EPS)


def norm_back(rows, r, gain, grad):
    lead = gain * grad
    return r * (lead - rows * (r * r) * jnp.mean(lead * rows, axis=-1, keepdims=True))


def gain_grad(gain, *pairs):
    total = sum(jnp.sum(w.astype(F32) * g, axis=1) for w, g in pairs)
    return total / gain.astype(F32)


def on_device(
    dp,
    ctx,
    layer_in,
    out_grad,
    first_gain,
    query_weight,
    key_weight,
    value_weight,
    output_weight,
    second_gain,
    gate_weight,
    up_weight,
    down_weight,
):
    plan, pair = Plan(dp, ctx), Pair(dp)
    _, local, width = layer_in.shape
    ff = gate_weight.shape[1]
    heads, group_width = HEADS // plan.groups, width // plan.groups
    place = jnp.stack([pair.me, plan.group()]).astype(jnp.int32)

    gains_given = jnp.stack([first_gain, second_gain], 1)
    gains_full, w_key, w_value, w_query = finish(
        *[
            Chain("weights", pair.gather(w))
            for w in (gains_given, key_weight, value_weight, query_weight)
        ]
    )
    gains_full = pair.join(gains_full, 0)
    gain_one = gains_full[:, 0].astype(F32)
    x = layer_in.reshape(local, width).astype(F32)
    r1 = scaled(x)
    h1 = (x * r1 * gain_one).astype(BF16)

    def project(w):
        return pair.times(h1, 1, w, lambda a, b: dotg(b, a, 0, 1)).astype(BF16)

    keys, values, query = project(w_key), project(w_value), project(w_query)

    def by_token(value):
        return [value[:, i * local : (i + 1) * local] for i in range(plan.groups)]

    paired = jnp.concatenate(
        [a.reshape(HEADS, HEAD_DIM, local) for a in (keys, values)], axis=1
    ).reshape(2 * width, local)
    order = Order(place)
    kv = Chain("kv", plan.exchange(plan.group_pieces(paired)))
    qs = Chain("qs", plan.exchange(plan.group_pieces(query)))
    later = [
        Chain("weights", pair.gather(w))
        for w in (output_weight, gate_weight, up_weight, down_weight)
    ]
    order([], [kv])
    order([], later[:2])
    order(later[:2], later[2:])
    order(later[2:] + [kv], [qs])
    weights = finish(*later)
    kv = jnp.concatenate(finish(kv)[0], axis=1)
    gather = [
        Chain("keys", plan.gather_rest(kv[2 * HEAD_DIM * h : 2 * HEAD_DIM * (h + 1)]))
        for h in range(heads)
    ]
    spread = [Chain("spread", plan.send_group(h1, i)) for i in range(1, plan.groups)]
    order([], gather[:2])
    for step in range(1, plan.bits):
        order(gather[:1], gather[:1])
    q = jnp.concatenate(finish(qs)[0], axis=1)
    outs = []
    for h in range(heads):
        (sources,) = finish(gather[h])
        coming = gather[h + 1 : h + 2] if plan.bits > 1 else []
        near = spread[:2] if h == 0 else spread[2:] if h == 2 else []
        q, sources, outs = order(
            coming + (spread[h - 1 : h] if h else []), coming + gather[h + 2 : h + 3] + near, (q, sources, outs)
        )
        gather[h].result = sources
        outs = outs + [attend(h, q, sources)]
    o_wide, o_low, lse = zip(*outs)
    sources = [c.result for c in gather]
    mixed = Chain("mixed", plan.exchange(by_token(jnp.concatenate(o_low, axis=0))))
    order([], [mixed])
    order(spread, [mixed])
    mixed = mixed.result
    dy = out_grad.reshape(local, width)
    kept, do_pieces = middle(
        place, layer_in.reshape(local, width), dy, gains_full[:, 1], mixed, weights, ff
    )
    layer_out, dy1, mixed, h2, hidden, d_gate, d_up, da = kept
    d_mixed = [
        Chain("d_mixed", plan.send_group(p, s)) for s, p in enumerate(do_pieces) if s
    ]
    order([], d_mixed)
    order(d_mixed, [])
    do = jnp.concatenate(do_pieces[:1] + finish(*d_mixed), axis=1)
    back = lambda h, do: attend_back(h, q, do, o_wide[h], lse[h], sources[h])
    grads = lambda *terms: plan.sum_rows(pair, weight_grads(place, dp, terms))
    hidden, h2, mixed = order([], [], (hidden, h2, mixed))
    downs = Chain("downs", grads((hidden, 1, dy)))
    order([], [downs])
    gates = Chain("gates", grads((h2, 1, d_gate)))
    order([], [gates])
    do = order([downs], [downs], do)
    dq0, pair0 = back(0, do)
    k0 = Chain("k0", plan.scatter_rest(pair0))
    dq0, d_up = order([gates], [k0, gates], (dq0, d_up))
    ups = Chain("ups", grads((h2, 1, d_up), (mixed, 0, da)))
    order([], [ups])
    do, dq0 = order([downs], [downs], (do, dq0))
    dq1, pair1 = back(1, do)
    k1 = Chain("k1", plan.scatter_rest(pair1))
    do, dq1 = order([downs, gates, k0, ups], [downs, gates, k0, k1, ups], (do, dq1))
    dq2, pair2 = back(2, do)
    k2 = Chain("k2", plan.scatter_rest(pair2))
    dq2 = order([downs, gates, k0, k1], [k0, k2, gates, downs, k1], dq2)
    (pair0,) = finish(k0)
    order([k2], [k2])
    order([gates, downs], [gates, downs])
    order([ups], [ups])
    pair1, pair2 = finish(k1, k2)
    rows = [h1] + finish(*spread)
    third = Chain(
        "third",
        plan.sum_heads(
            pair,
            head_grads(place, dp, (dq0, dq1, dq2), (pair0, pair1, pair2), rows),
            heads * HEAD_DIM,
        ),
    )
    d_first = Chain("d_first", plan.exchange(by_token(jnp.concatenate([dq0, pair0], axis=0))))
    d_last = Chain(
        "d_last", plan.exchange(by_token(jnp.concatenate([dq1, dq2, pair1, pair2], axis=0)))
    )
    order([], [third])
    order([third, gates, downs], [third, gates, downs])
    order([ups], [ups])
    order([third], [third])
    order([gates, downs], [gates, downs])
    order([ups], [ups])
    order([third], [third])
    order([gates, downs], [gates, downs])
    order([ups], [ups])
    order([third], [third])
    order([gates], [gates])
    order([ups], [ups])
    order([], [d_first])
    order([third], [third])
    order([gates], [gates])
    order([ups], [ups])
    order([d_first], [d_last])
    order([third], [third])
    order([ups], [ups])
    first, last = (
        plan.natural(c).reshape(plan.groups, -1, local) for c in finish(d_first, d_last)
    )
    first = first.reshape(plan.groups, -1, HEAD_DIM, local)
    last = last.reshape(plan.groups, -1, HEAD_DIM, local)
    whole = lambda a, b, c: jnp.stack([first[:, a], last[:, b], last[:, c]], 1).reshape(width, local)
    d_query, d_key, d_value = whole(0, 0, 1), whole(1, 2, 4), whole(2, 3, 5)
    order([third, gates, ups, downs, d_last], [])
    pair.me = order.token[0]
    dh1 = pair.join(
        [
            dotg(d_query, a, 0, 1) + dotg(d_key, b, 0, 1) + dotg(d_value, c, 0, 1)
            for a, b, c in zip(w_query, w_key, w_value)
        ],
        1,
    )
    back_one = norm_back(x, r1, gain_one, dh1)
    in_grad = (back_one + dy1).astype(BF16).reshape(layer_in.shape)

    third, downs, gates, ups = (
        v.astype(F32) for v in finish(third, downs, gates, ups)
    )
    d_wq, d_wk, d_wv = (third[:, i * width : (i + 1) * width] for i in range(3))
    d_gate, d_up = gates, ups[:, :ff]
    return (
        layer_out.reshape(layer_in.shape),
        in_grad,
        gain_grad(
            first_gain, (query_weight, d_wq), (key_weight, d_wk), (value_weight, d_wv)
        ),
        d_wq,
        d_wk,
        d_wv,
        ups[:, ff:],
        gain_grad(second_gain, (gate_weight, d_gate), (up_weight, d_up)),
        d_gate,
        d_up,
        downs,
    )


def solution(mesh):
    tokens, matrix, vector = P("dp", "ctx", None), P("dp", None), P("dp")
    weights = (vector, matrix, matrix, matrix, matrix, vector, matrix, matrix, matrix)
    return jax.shard_map(
        functools.partial(on_device, mesh.shape["dp"], mesh.shape["ctx"]),
        mesh=mesh,
        in_specs=(tokens, tokens) + weights,
        out_specs=(tokens, tokens) + weights,
        check_vma=False,
    )
```

```python
import functools
import math

import jax
import jax.numpy as jnp
from jax import lax
from jax.experimental import pallas as pl
from jax.experimental.pallas import tpu as pltpu
from jax.sharding import PartitionSpec as P

HEADS = 12
HEAD_DIM = 64
EPS = 1e-06
LOG2E = 1.4426950408889634
SCALE = HEAD_DIM ** (-0.5)
AXES = ("dp", "ctx")
F32 = jnp.float32
BF16 = jnp.bfloat16


def dotg(a, b, ca, cb):
    return lax.dot_general(a, b, (((ca,), (cb,)), ((), ())), preferred_element_type=F32)


def attend_kernel(key_block, q_ref, *refs):
    sources = refs[:-3]
    o_ref, low_ref, lse_ref = refs[-3:]
    tokens = q_ref.shape[1]
    query = q_ref[...] * BF16(SCALE)
    top = jnp.full((1, tokens), -jnp.inf, F32)
    total = jnp.zeros((1, tokens), F32)
    acc = jnp.zeros((HEAD_DIM, tokens), F32)
    for source in sources:
        for at in range(0, source.shape[1], key_block):
            ks = slice(at, at + key_block)
            scores = dotg(source[:HEAD_DIM, ks], query, 0, 0) * LOG2E
            new_top = jnp.maximum(top, jnp.max(scores, axis=0, keepdims=True))
            decay = jnp.exp2(top - new_top)
            probs = jnp.exp2(scores - new_top)
            total = total * decay + jnp.sum(probs, axis=0, keepdims=True)
            acc = acc * decay + jnp.dot(
                source[HEAD_DIM:, ks], probs.astype(BF16), preferred_element_type=F32
            )
            top = new_top
    out = acc / total
    o_ref[...] = out
    low_ref[...] = out.astype(BF16)
    lse_ref[...] = top + jnp.log2(total)


def cost(flops, nbytes):
    return pl.CostEstimate(flops=flops * 10, transcendentals=0, bytes_accessed=nbytes)


def attend(head, query, sources, key_block=1024):
    tokens = query.shape[1]
    keys = sum(s.shape[1] for s in sources)
    whole = lambda s: pl.BlockSpec(s.shape, lambda i: (0, 0))
    flat = lambda rows: pl.BlockSpec((rows, tokens), lambda i: (0, 0))
    return pl.pallas_call(
        functools.partial(attend_kernel, key_block),
        grid=(1,),
        in_specs=[pl.BlockSpec((HEAD_DIM, tokens), lambda i: (head, 0))]
        + [whole(s) for s in sources],
        out_specs=(flat(HEAD_DIM), flat(HEAD_DIM), flat(1)),
        out_shape=(
            jax.ShapeDtypeStruct((HEAD_DIM, tokens), F32),
            jax.ShapeDtypeStruct((HEAD_DIM, tokens), BF16),
            jax.ShapeDtypeStruct((1, tokens), F32),
        ),
        compiler_params=pltpu.CompilerParams(vmem_limit_bytes=60 << 20),
        cost_estimate=cost(4 * 4 * HEAD_DIM * tokens * keys, 0),
        name="attend",
    )(query, *sources)


def attend_back_kernel(key_block, n, q_ref, do_ref, o_ref, lse_ref, *refs):
    sources, dq_ref, outs = refs[:n], refs[n], refs[n + 1 :]
    query = q_ref[...] * BF16(SCALE)
    grad = do_ref[...]
    lse = lse_ref[...]
    delta = jnp.sum(grad.astype(F32) * o_ref[...], axis=0, keepdims=True)
    dq = jnp.zeros(query.shape, F32)
    tokens = sources[0].shape[1]
    for i, source in enumerate(sources):
        out, base = outs[i * len(outs) // n], i % (n // len(outs)) * tokens
        for at in range(0, tokens, key_block):
            ks = slice(at, at + key_block)
            to = slice(base + at, base + at + key_block)
            keys, values = source[:HEAD_DIM, ks], source[HEAD_DIM:, ks]
            probs = jnp.exp2(dotg(keys, query, 0, 0) * LOG2E - lse)
            gap = dotg(values, grad, 0, 0) - delta
            low = probs.astype(BF16)
            ds = (probs * gap).astype(BF16)
            out[HEAD_DIM:, to] = dotg(grad, low, 1, 1).astype(BF16)
            out[:HEAD_DIM, to] = dotg(query, ds, 1, 1).astype(BF16)
            dq = dq + jnp.dot(keys, ds, preferred_element_type=F32)
    dq_ref[...] = (dq * SCALE).astype(BF16)


def attend_back(head, query, grad, out, lse, sources, key_block=256):
    tokens = query.shape[1]
    n = len(sources)
    parts = min(n, 2)
    keys = sum(s.shape[1] for s in sources)
    whole = lambda s: pl.BlockSpec(s.shape, lambda i: (0, 0))
    mine = lambda: pl.BlockSpec((HEAD_DIM, tokens), lambda i: (head, 0))
    shapes = (jax.ShapeDtypeStruct((HEAD_DIM, tokens), BF16),) + tuple(
        jax.ShapeDtypeStruct((2 * HEAD_DIM, keys // parts), BF16) for _ in range(parts)
    )
    outs = pl.pallas_call(
        functools.partial(attend_back_kernel, key_block, n),
        grid=(1,),
        in_specs=[mine(), mine(), whole(out), whole(lse)] + [whole(s) for s in sources],
        out_specs=tuple(whole(s) for s in shapes),
        out_shape=shapes,
        compiler_params=pltpu.CompilerParams(vmem_limit_bytes=60 << 20),
        cost_estimate=cost(4 * 10 * HEAD_DIM * tokens * keys, 0),
        name="attend_back",
    )(query, grad, out, lse, *sources)
    return outs[0], list(outs[1:])


def copies(pair, parts, full, sems):
    half = parts[0].shape[0]
    made = []
    for i, part in enumerate(parts):
        at = 0 if len(parts) == 1 else pl.multiple_of((pair ^ i) * half, half)
        made.append(pltpu.make_async_copy(part, full.at[pl.ds(at, half), :], sems.at[i]))
    return made


def middle_kernel(groups, parts, chunk, place_ref, x_ref, dy_ref, gain_ref, *refs):
    pieces = refs[:groups]
    given = refs[groups : groups + 4 * parts]
    rest = refs[groups + 4 * parts :]
    (out_ref, dy1_ref, mixed_ref, h2_ref, hidden_ref, dgate_ref, dup_ref, da_ref) = rest[:8]
    back_pieces = rest[8 : 8 + groups]
    wo, wg, wu, wd, do_ref, sems = rest[8 + groups :]
    pair, group = place_ref[0], place_ref[1]
    made = [
        copies(pair, given[j * parts : (j + 1) * parts], full, sems.at[j])
        for j, full in enumerate((wo, wg, wu, wd))
    ]
    for cs in made:
        for c in cs:
            c.start()
    rows = pieces[0].shape[0]
    spot = [pl.ds(pl.multiple_of((group ^ s) * rows, rows), rows) for s in range(groups)]
    for s in range(groups):
        mixed_ref[spot[s], :] = pieces[s][...]
    for c in made[0]:
        c.wait()
    dy = dy_ref[...]
    gain = gain_ref[...].astype(F32)
    y1 = x_ref[...].astype(F32) + dotg(mixed_ref[...], wo[...], 0, 0)
    r2 = lax.rsqrt(jnp.mean(y1 * y1, axis=-1, keepdims=True) + EPS)
    h2 = (y1 * r2 * gain).astype(BF16)
    h2_ref[...] = h2
    for cs in made[1:]:
        for c in cs:
            c.wait()
    result = y1
    dh2 = jnp.zeros(y1.shape, F32)
    root, cubic = math.sqrt(2 / math.pi), 0.044715
    for at in range(0, wg.shape[1], chunk):
        cs = slice(at, at + chunk)
        u = jnp.dot(h2, wg[:, cs], preferred_element_type=F32)
        upper = jnp.dot(h2, wu[:, cs], preferred_element_type=F32)
        square = u * u
        t = jnp.tanh(root * (u + cubic * (u * square)))
        share = 0.5 * (1.0 + t)
        bent = u * share
        slope = share + (0.5 * root) * u * (1.0 - t * t) * (1.0 + (3 * cubic) * square)
        hidden = (bent * upper).astype(BF16)
        hidden_ref[:, cs] = hidden
        result = result + jnp.dot(hidden, wd[cs, :], preferred_element_type=F32)
        dhidden = dotg(dy, wd[cs, :], 1, 1)
        dgate = (dhidden * upper * slope).astype(BF16)
        dup = (dhidden * bent).astype(BF16)
        dgate_ref[:, cs] = dgate
        dup_ref[:, cs] = dup
        dh2 = dh2 + dotg(dgate, wg[:, cs], 1, 1) + dotg(dup, wu[:, cs], 1, 1)
    out_ref[...] = result.astype(BF16)
    lead = gain * dh2
    mean = jnp.mean(lead * y1, axis=-1, keepdims=True)
    dy1 = dy.astype(F32) + r2 * (lead - y1 * (r2 * r2) * mean)
    dy1_ref[...] = dy1
    da = dy1.astype(BF16)
    da_ref[...] = da
    do_ref[...] = dotg(wo[...], da, 1, 1).astype(BF16)
    for s in range(groups):
        back_pieces[s][...] = do_ref[spot[s], :]


def middle(place, x, dy, gain, pieces, weights, ff):
    tokens, width = x.shape
    groups, parts = len(pieces), len(weights[0])
    vmem = pl.BlockSpec(memory_space=pltpu.VMEM)
    some = lambda shape, dtype: jax.ShapeDtypeStruct(shape, dtype)
    wide = some((tokens, ff), BF16)
    flat = some((tokens, width), BF16)
    outs = pl.pallas_call(
        functools.partial(middle_kernel, groups, parts, 512),
        in_specs=[pl.BlockSpec(memory_space=pltpu.SMEM)]
        + [vmem] * (3 + groups)
        + [pl.BlockSpec(memory_space=pl.ANY)] * (4 * parts),
        out_specs=(vmem,) * (8 + groups),
        out_shape=(
            flat,
            some((tokens, width), F32),
            some((width, tokens), BF16),
            flat,
            wide,
            wide,
            wide,
            flat,
        )
        + tuple(some(p.shape, BF16) for p in pieces),
        scratch_shapes=[
            pltpu.VMEM((width, width), BF16),
            pltpu.VMEM((width, ff), BF16),
            pltpu.VMEM((width, ff), BF16),
            pltpu.VMEM((ff, width), BF16),
            pltpu.VMEM((width, tokens), BF16),
            pltpu.SemaphoreType.DMA((4, parts)),
        ],
        compiler_params=pltpu.CompilerParams(vmem_limit_bytes=60 << 20),
        cost_estimate=cost(4 * tokens * width * (width + 3 * ff), 6 * width * ff),
        name="middle",
    )(place, x, dy, gain.reshape(1, width), *pieces, *[p for w in weights for p in w])
    return outs[:8], list(outs[8:])


def grads_kernel(parts, axes, place_ref, *refs):
    n = len(axes)
    lefts, rights, outs = refs[:n], refs[n : 2 * n], refs[2 * n :]
    for i, out in enumerate(outs):
        base = 0
        for left, right, axis in zip(lefts, rights, axes):
            rows, to = left.shape[axis] // parts, slice(base, base + right.shape[1])
            at = pl.multiple_of((place_ref[0] ^ i) * rows, rows) if parts > 1 else 0
            part = left[:, pl.ds(at, rows)] if axis == 1 else left[pl.ds(at, rows), :]
            value = dotg(part, right[...], 1 - axis, 0).astype(BF16)
            if parts == 1:
                out[:, to] = value
            else:
                size = out.shape[1]
                for b in range(out.shape[0]):
                    out[b ^ place_ref[2 + i], :, to] = value[b * size : (b + 1) * size, :]
            base += right.shape[1]


def weight_grads(place, dp, ctx, terms):
    parts = 2 if dp == 2 else 1
    lefts, axes, rights = zip(*terms)
    rows = lefts[0].shape[axes[0]] // parts
    columns = sum(r.shape[1] for r in rights)
    shape = (ctx, rows // ctx, columns) if parts == 2 else (rows, columns)
    vmem = pl.BlockSpec(memory_space=pltpu.VMEM)
    return pl.pallas_call(
        functools.partial(grads_kernel, parts, axes),
        in_specs=[pl.BlockSpec(memory_space=pltpu.SMEM)] + [vmem] * (2 * len(terms)),
        out_specs=(vmem,) * parts,
        out_shape=(jax.ShapeDtypeStruct(shape, BF16),) * parts,
        compiler_params=pltpu.CompilerParams(vmem_limit_bytes=60 << 20),
        cost_estimate=cost(2 * parts * rows * columns * rights[0].shape[0], 0),
        name="weight_grads",
    )(place, *lefts, *rights)


def ordered_kernel(n, given, code_ref, near_ref, far_ref, *refs):
    weights, outs, sums = refs[:given], refs[given : given + n], refs[given + n :]
    half, size = near_ref.shape[:2]

    def put(block, rows):
        base, total = 0, jnp.zeros((size, 1), F32)
        for i, out in enumerate(outs):
            value = block[:, base : base + out.shape[1]].astype(F32)
            out[rows, :] = value
            base += out.shape[1]
            if i < given:
                product = value * weights[i][rows, :].astype(F32)
                total = total + jnp.sum(product, axis=1, keepdims=True)
        for s in sums:
            s[rows, :] = total

    for b in range(2 * half):
        at = b ^ code_ref[2]
        rows = slice(b * size, (b + 1) * size)
        pl.when(at < half)(
            lambda at=at, rows=rows: put(near_ref[jnp.minimum(at, half - 1)], rows)
        )
        pl.when(at >= half)(
            lambda at=at, rows=rows: put(far_ref[jnp.maximum(at - half, 0)], rows)
        )


def ordered(place, near, far, columns, weights=()):
    rows = 2 * near.shape[0] * near.shape[1]
    vmem = pl.BlockSpec(memory_space=pltpu.VMEM)
    shapes = [jax.ShapeDtypeStruct((rows, c), F32) for c in columns]
    shapes += [jax.ShapeDtypeStruct((rows, 1), F32)] * min(len(weights), 1)
    return pl.pallas_call(
        functools.partial(ordered_kernel, len(columns), len(weights)),
        in_specs=[pl.BlockSpec(memory_space=pltpu.SMEM)] + [vmem] * (2 + len(weights)),
        out_specs=(vmem,) * len(shapes),
        out_shape=tuple(shapes),
        compiler_params=pltpu.CompilerParams(vmem_limit_bytes=60 << 20),
        cost_estimate=cost(near.size, 0),
        name="ordered",
    )(place, near, far, *weights)


def head_grads_kernel(heads, devices, parts, place_ref, *refs):
    outs = refs[-parts:]
    queries, pairs = refs[:heads], refs[heads : 2 * heads]
    rows = refs[2 * heads : -parts]
    d = jnp.concatenate(
        [q[...] for q in queries]
        + [p[:HEAD_DIM, :] for p in pairs]
        + [p[HEAD_DIM:, :] for p in pairs],
        axis=0,
    )
    width = rows[0].shape[1] // parts
    for i, out in enumerate(outs):
        at = pl.multiple_of((place_ref[0] ^ i) * width, width) if parts > 1 else 0
        left = jnp.concatenate([r[:, pl.ds(at, width)] for r in rows], axis=0)
        out[...] = jnp.dot(d, left, preferred_element_type=F32).T.astype(BF16)


def head_grads(place, dp, queries, pairs, rows):
    heads, parts = len(queries), 2 if dp == 2 else 1
    width, columns = rows[0].shape[1], 3 * HEAD_DIM * heads
    vmem = pl.BlockSpec(memory_space=pltpu.VMEM)
    return pl.pallas_call(
        functools.partial(head_grads_kernel, heads, dp, parts),
        in_specs=[pl.BlockSpec(memory_space=pltpu.SMEM)] + [vmem] * (2 * heads + len(rows)),
        out_specs=(vmem,) * parts,
        out_shape=(jax.ShapeDtypeStruct((width // parts, columns), BF16),) * parts,
        compiler_params=pltpu.CompilerParams(vmem_limit_bytes=60 << 20),
        cost_estimate=cost(2 * queries[0].shape[1] * width * columns, 0),
        name="head_grads",
    )(place, *queries, *pairs, *rows)


def unstacked(value, base, rows, cols):
    n = cols // LANES
    part = value[base : base + rows * n].reshape(n, rows, LANES)
    return part.transpose(1, 0, 2).reshape(rows, cols).astype(F32)


class Plan:
    def __init__(self, dp, ctx):
        self.dp, self.ctx = dp, ctx
        self.groups = math.gcd(HEADS, ctx)
        self.rest = ctx // self.groups
        self.bits = self.rest.bit_length() - 1
        self.group_bits = self.groups.bit_length() - 1
        assert 1 << self.bits == self.rest and self.groups & (self.groups - 1) == 0

    def bit(self, parity, step):
        return step if parity == 0 else self.bits - 1 - step

    def rest_perm(self, step):
        return [
            (d * self.ctx + c, d * self.ctx + (c ^ (1 << self.bit(d % 2, step))))
            for d in range(self.dp)
            for c in range(self.ctx)
        ]

    def group_perm(self, s):
        return [(c, c ^ (s * self.rest)) for c in range(self.ctx)]

    def group(self):
        return lax.axis_index("ctx") // self.rest

    def my_bit(self, step, other=0):
        c = lax.axis_index("ctx")
        even = (c >> self.bit(0, step)) & 1
        odd = (c >> self.bit(1, step)) & 1
        return jnp.where((lax.axis_index("dp") + other) % 2 == 0, even, odd)

    def over_rest(self, value, step):
        return lax.ppermute(value, AXES, self.rest_perm(step))

    def over_group(self, value, s):
        return value if s == 0 else lax.ppermute(value, "ctx", self.group_perm(s))

    def gather_rest(self, value):
        blocks = [value]
        for step in range(self.bits):
            came = yield [
                (b, lambda v, step=step: self.over_rest(v, step)) for b in blocks
            ]
            blocks = blocks + came
        return blocks

    def natural(self, pieces, axis=0):
        g = self.group()
        step = 1
        while step < self.groups:
            odd = (g & step) != 0
            pieces = [
                jnp.where(odd, pieces[i ^ step], pieces[i]) for i in range(self.groups)
            ]
            step *= 2
        return jnp.concatenate(pieces, axis=axis)

    def hop(self, step):
        if step < self.bits:
            return lambda v: self.over_rest(v, step)
        return lambda v: self.over_group(v, 1 << (step - self.bits))

    def place_bit(self, step, other=0):
        if step < self.bits:
            return self.my_bit(step, other)
        return (self.group() >> (step - self.bits)) & 1

    def halves(self, value, step):
        half = value.shape[0] // 2
        b = self.place_bit(step)
        return (
            lax.dynamic_slice_in_dim(value, b * half, half, 0),
            lax.dynamic_slice_in_dim(value, (1 - b) * half, half, 0),
        )

    def group_pieces(self, value):
        size = value.shape[0] // self.groups
        return [
            lax.dynamic_slice_in_dim(value, (self.group() ^ s) * size, size, 0)
            for s in range(self.groups)
        ]

    def to_rest(self, value, step):
        return [(value, lambda v: self.over_rest(v, step))]

    def to_groups(self, pieces):
        return [
            (p, lambda v, s=s: self.over_group(v, s)) for s, p in enumerate(pieces) if s
        ]

    def exchange(self, pieces):
        came = yield self.to_groups(pieces)
        return [pieces[0]] + came

    def send_group(self, value, s):
        came = yield [(value, lambda v: self.over_group(v, s))]
        return came[0]

    def scatter_rest(self, parts):
        for step in reversed(range(self.bits)):
            if step < self.bits - 1:
                half = parts.shape[1] // 2
                parts = parts[:, :half], parts[:, half:]
            came = yield self.to_rest(parts[1], step)
            parts = add_low(parts[0], came[0])
        return parts if self.bits else parts[0]

    def reduce_rows(self, value, steps):
        for step in range(steps):
            kept, gone = self.halves(value, step)
            came = yield [(gone, self.hop(step))]
            value = add_low(kept, came[0])
        return value

    def expand_rows(self, value, steps):
        for step in reversed(range(steps)):
            came = yield [(value, self.hop(step))]
            value = jnp.where(
                self.place_bit(step) == 0,
                jnp.concatenate([value, came[0]], axis=0),
                jnp.concatenate([came[0], value], axis=0),
            )
        return value

    def code(self, other):
        steps = self.bits + self.group_bits
        total = 0
        for step in range(steps):
            total = total + (self.place_bit(step, other) << (steps - 1 - step))
        return total

    def sum_blocks(self, pair, stacks):
        steps = self.bits + self.group_bits
        terms = yield from pair.combine(stacks)
        for step in range(steps):
            half = terms[0].shape[0] // 2
            came = yield [(total_low([t[half:] for t in terms]), self.hop(step))]
            terms = [t[:half] for t in terms] + came
        value = total_low(terms)
        for step in reversed(range(steps)):
            came = yield [(value, self.hop(step))]
            halves = [value] + came
            value = jnp.concatenate(halves, axis=0) if step else halves
        return value

    def sum_rows(self, pair, stacks):
        terms = yield from pair.combine(stacks)
        value = yield from self.reduce_rows(total_low(terms), self.bits + self.group_bits)
        return (yield from self.expand_rows(value, self.bits + self.group_bits))

    def sum_heads(self, pair, stacks, columns):
        terms = yield from pair.combine(stacks)
        value = yield from self.reduce_rows(total_low(terms), self.bits)
        rows, groups = value.shape[0], [value]
        for step in range(self.group_bits):
            came = yield [(jnp.concatenate(groups, axis=0), self.hop(self.bits + step))]
            groups = groups + [
                came[0][i * rows : (i + 1) * rows] for i in range(len(groups))
            ]
        value = jnp.concatenate(
            [
                self.natural([p[:, at : at + columns] for p in groups], 1)
                for at in range(0, value.shape[1], columns)
            ],
            axis=1,
        )
        return (yield from self.expand_rows(value, self.bits))


def add_low(a, b):
    return (a.astype(F32) + b.astype(F32)).astype(BF16)


def total_low(terms):
    return functools.reduce(jnp.add, [t.astype(F32) for t in terms]).astype(BF16)


class Chain:
    def __init__(self, name, stages):
        self.name, self.stages, self.came, self.result = name, stages, None, None
        self.stage = 0

    def send(self, moves, values):
        self.stage += 1
        with jax.named_scope(f"{self.name}_{self.stage}"):
            self.came = [move(v) for v, (_, move) in zip(values, moves)]

    def next_moves(self):
        if self.result is not None:
            return []
        try:
            return self.stages.send(self.came)
        except StopIteration as end:
            self.came, self.result = None, end.value
            return []


class Order:
    def __init__(self, token):
        self.token = token

    def __call__(self, land, launch, values=()):
        moves = [c.next_moves() for c in launch]
        waiting = [c for c in land if c not in launch and c.came is not None]
        ended = [c for c in launch if c.result is not None]
        self.token, values, held, done, sent = lax.optimization_barrier(
            (
                self.token,
                values,
                [c.came for c in waiting],
                [c.result for c in ended],
                [[v for v, _ in m] for m in moves],
            )
        )
        for c, came in zip(waiting, held):
            c.came = came
        for c, result in zip(ended, done):
            c.result = result
        for c, m, vs in zip(launch, moves, sent):
            if m:
                c.send(m, vs)
        return values


def finish(*chains):
    while any(c.result is None for c in chains):
        for c in chains:
            m = c.next_moves()
            if m:
                c.send(m, [v for v, _ in m])
    return [c.result for c in chains]


def add_low(a, b):
    return (a.astype(F32) + b.astype(F32)).astype(BF16)


def total_low(terms):
    return functools.reduce(jnp.add, [t.astype(F32) for t in terms]).astype(BF16)


class Pair:
    def __init__(self, dp):
        self.dp = dp
        self.me = lax.axis_index("dp")

    def swap(self, value):
        return lax.ppermute(value, "dp", [(0, 1), (1, 0)])

    def gather(self, weight):
        if self.dp != 2:
            return [lax.all_gather(weight, "dp", axis=0, tiled=True)]
        came = yield [(weight, self.swap)]
        return [weight] + came

    def part(self, value, i, axis):
        if self.dp != 2:
            return value
        half = value.shape[axis] // 2
        at = jnp.where(self.me == i, 0, half)
        return lax.dynamic_slice_in_dim(value, at, half, axis)

    def join(self, parts, axis):
        if len(parts) == 1:
            return parts[0]
        return jnp.where(
            self.me == 0,
            jnp.concatenate(parts, axis),
            jnp.concatenate(parts[::-1], axis),
        )

    def times(self, value, axis, weight, contract):
        return functools.reduce(
            jnp.add,
            [
                contract(self.part(value, i, axis), w)
                for i, w in enumerate(weight)
            ],
        )

    def combine(self, stacks):
        if self.dp == 2:
            came = yield [(stacks[1], self.swap)]
            return [stacks[0]] + came
        return [lax.psum_scatter(stacks[0], "dp", scatter_dimension=0, tiled=True)]


def scaled(rows):
    return lax.rsqrt(jnp.mean(rows * rows, axis=-1, keepdims=True) + EPS)


def norm_back(rows, r, gain, grad):
    lead = gain * grad
    return r * (lead - rows * (r * r) * jnp.mean(lead * rows, axis=-1, keepdims=True))


def gain_grad(gain, *pairs):
    total = sum(jnp.sum(w.astype(F32) * g, axis=1) for w, g in pairs)
    return total / gain.astype(F32)


def on_device(
    dp,
    ctx,
    layer_in,
    out_grad,
    first_gain,
    query_weight,
    key_weight,
    value_weight,
    output_weight,
    second_gain,
    gate_weight,
    up_weight,
    down_weight,
):
    plan, pair = Plan(dp, ctx), Pair(dp)
    _, local, width = layer_in.shape
    ff = gate_weight.shape[1]
    heads, group_width = HEADS // plan.groups, width // plan.groups
    place = jnp.stack([pair.me, plan.group(), plan.code(0), plan.code(1)]).astype(jnp.int32)

    gains_given = jnp.stack([first_gain, second_gain], 1)
    gains_full, w_key, w_value, w_query = finish(
        *[
            Chain("weights", pair.gather(w))
            for w in (gains_given, key_weight, value_weight, query_weight)
        ]
    )
    gains_full = pair.join(gains_full, 0)
    gain_one = gains_full[:, 0].astype(F32)
    x = layer_in.reshape(local, width).astype(F32)
    r1 = scaled(x)
    h1 = (x * r1 * gain_one).astype(BF16)

    def project(w):
        return pair.times(h1, 1, w, lambda a, b: dotg(b, a, 0, 1)).astype(BF16)

    keys, values, query = project(w_key), project(w_value), project(w_query)

    def by_token(value):
        return [value[:, i * local : (i + 1) * local] for i in range(plan.groups)]

    paired = jnp.concatenate(
        [a.reshape(HEADS, HEAD_DIM, local) for a in (keys, values)], axis=1
    ).reshape(2 * width, local)
    order = Order(place)
    kv = Chain("kv", plan.exchange(plan.group_pieces(paired)))
    qs = Chain("qs", plan.exchange(plan.group_pieces(query)))
    later = [
        Chain("weights", pair.gather(w))
        for w in (output_weight, gate_weight, up_weight, down_weight)
    ]
    order([], [kv])
    order([], later[:2])
    order(later[:2], later[2:])
    order(later[2:] + [kv], [qs])
    weights = finish(*later)
    kv = jnp.concatenate(finish(kv)[0], axis=1)
    gather = [
        Chain("keys", plan.gather_rest(kv[2 * HEAD_DIM * h : 2 * HEAD_DIM * (h + 1)]))
        for h in range(heads)
    ]
    spread = [Chain("spread", plan.send_group(h1, i)) for i in range(1, plan.groups)]
    order([], gather[:2])
    for step in range(1, plan.bits):
        order(gather[:1], gather[:1])
    q = jnp.concatenate(finish(qs)[0], axis=1)
    outs = []
    for h in range(heads):
        (sources,) = finish(gather[h])
        coming = gather[h + 1 : h + 2] if plan.bits > 1 else []
        near = spread[:2] if h == 0 else spread[2:] if h == 2 else []
        q, sources, outs = order(
            coming + (spread[h - 1 : h] if h else []), coming + gather[h + 2 : h + 3] + near, (q, sources, outs)
        )
        gather[h].result = sources
        outs = outs + [attend(h, q, sources)]
    o_wide, o_low, lse = zip(*outs)
    sources = [c.result for c in gather]
    mixed = Chain("mixed", plan.exchange(by_token(jnp.concatenate(o_low, axis=0))))
    order([], [mixed])
    order(spread, [mixed])
    mixed = mixed.result
    dy = out_grad.reshape(local, width)
    kept, do_pieces = middle(
        place, layer_in.reshape(local, width), dy, gains_full[:, 1], mixed, weights, ff
    )
    layer_out, dy1, mixed, h2, hidden, d_gate, d_up, da = kept
    d_mixed = [
        Chain("d_mixed", plan.send_group(p, s)) for s, p in enumerate(do_pieces) if s
    ]
    order([], d_mixed)
    order(d_mixed, [])
    do = jnp.concatenate(do_pieces[:1] + finish(*d_mixed), axis=1)
    back = lambda h, do: attend_back(h, q, do, o_wide[h], lse[h], sources[h])

    def grads(*terms):
        stacks = weight_grads(place, dp, ctx, terms)
        return plan.sum_blocks(pair, stacks) if dp == 2 else plan.sum_rows(pair, stacks)

    hidden, h2, mixed = order([], [], (hidden, h2, mixed))
    downs = Chain("downs", grads((hidden, 1, dy)))
    order([], [downs])
    gates = Chain("gates", grads((h2, 1, d_gate)))
    order([], [gates])
    ups = Chain("ups", grads((h2, 1, d_up), (mixed, 0, da)))
    order([], [ups])
    do = order([downs], [downs], do)
    dq0, pair0 = back(0, do)
    k0 = Chain("k0", plan.scatter_rest(pair0))
    do, dq0 = order([downs, gates], [downs, gates, k0], (do, dq0))
    dq1, pair1 = back(1, do)
    k1 = Chain("k1", plan.scatter_rest(pair1))
    do, dq1 = order([downs, gates, k0, ups], [downs, gates, k0, k1, ups], (do, dq1))
    dq2, pair2 = back(2, do)
    k2 = Chain("k2", plan.scatter_rest(pair2))
    dq2 = order([downs, gates, k0, k1], [k0, k2, gates, downs, k1], dq2)
    (pair0,) = finish(k0)
    order([k2], [k2])
    order([gates, downs], [gates, downs])
    order([ups], [ups])
    pair1, pair2 = finish(k1, k2)
    rows = [h1] + finish(*spread)
    third = Chain(
        "third",
        plan.sum_heads(
            pair,
            head_grads(place, dp, (dq0, dq1, dq2), (pair0, pair1, pair2), rows),
            heads * HEAD_DIM,
        ),
    )
    d_first = Chain("d_first", plan.exchange(by_token(jnp.concatenate([dq0, pair0], axis=0))))
    d_last = Chain(
        "d_last", plan.exchange(by_token(jnp.concatenate([dq1, dq2, pair1, pair2], axis=0)))
    )
    order([], [third])
    order([third, gates, downs], [third, gates, downs])
    order([ups], [ups])
    order([third], [third])
    order([gates, downs], [gates, downs])
    order([ups], [ups])
    order([third], [third])
    order([gates, downs], [gates, downs])
    order([ups], [ups])
    order([third], [third])
    order([gates], [gates])
    order([ups], [ups])
    order([ups], [ups])
    order([], [d_first])
    order([third], [third])
    order([gates], [gates])
    order([ups], [ups])
    order([d_first], [d_last])
    order([third], [third])
    order([d_last], [])
    first, last = (
        plan.natural(c).reshape(plan.groups, -1, local) for c in finish(d_first, d_last)
    )
    first = first.reshape(plan.groups, -1, HEAD_DIM, local)
    last = last.reshape(plan.groups, -1, HEAD_DIM, local)
    whole = lambda a, b, c: jnp.stack([first[:, a], last[:, b], last[:, c]], 1).reshape(width, local)
    d_query, d_key, d_value = whole(0, 0, 1), whole(1, 2, 4), whole(2, 3, 5)
    dh1 = pair.join(
        [
            dotg(d_query, a, 0, 1) + dotg(d_key, b, 0, 1) + dotg(d_value, c, 0, 1)
            for a, b, c in zip(w_query, w_key, w_value)
        ],
        1,
    )
    back_one = norm_back(x, r1, gain_one, dh1)
    in_grad = (back_one + dy1).astype(BF16).reshape(layer_in.shape)

    (third,) = finish(third)
    third = third.astype(F32)
    d_wq, d_wk, d_wv = (third[:, i * width : (i + 1) * width] for i in range(3))
    gain_one_grad = gain_grad(
        first_gain, (query_weight, d_wq), (key_weight, d_wk), (value_weight, d_wv)
    )
    downs, gates = finish(downs, gates)
    if dp == 2:
        (downs,) = ordered(place, *downs, [width])
        d_gate, total = ordered(place, *gates, [ff], (gate_weight,))
    else:
        downs, d_gate = downs.astype(F32), gates.astype(F32)
    early = (in_grad, downs, d_gate, d_wq, d_wk, d_wv, gain_one_grad)
    in_grad, downs, d_gate, d_wq, d_wk, d_wv, gain_one_grad = order([], [], early)
    order([ups], [])
    place = order.token
    (ups,) = finish(ups)
    if dp == 2:
        d_up, d_wo, rest = ordered(place, *ups, [ff, width], (up_weight,))
        gain_two_grad = (total + rest)[:, 0] / second_gain.astype(F32)
    else:
        ups = ups.astype(F32)
        d_up, d_wo = ups[:, :ff], ups[:, ff:]
        gain_two_grad = gain_grad(second_gain, (gate_weight, d_gate), (up_weight, d_up))
    return (
        layer_out.reshape(layer_in.shape),
        in_grad,
        gain_one_grad,
        d_wq,
        d_wk,
        d_wv,
        d_wo,
        gain_two_grad,
        d_gate,
        d_up,
        downs,
    )


def solution(mesh):
    tokens, matrix, vector = P("dp", "ctx", None), P("dp", None), P("dp")
    weights = (vector, matrix, matrix, matrix, matrix, vector, matrix, matrix, matrix)
    return jax.shard_map(
        functools.partial(on_device, mesh.shape["dp"], mesh.shape["ctx"]),
        mesh=mesh,
        in_specs=(tokens, tokens) + weights,
        out_specs=(tokens, tokens) + weights,
        check_vma=False,
    )
```

```python
import functools
import math

import jax
import jax.numpy as jnp
from jax import lax
from jax.experimental import pallas as pl
from jax.experimental.pallas import tpu as pltpu
from jax.sharding import PartitionSpec as P

HEADS = 12
HEAD_DIM = 64
EPS = 1e-06
LOG2E = 1.4426950408889634
SCALE = HEAD_DIM ** (-0.5)
AXES = ("dp", "ctx")
F32 = jnp.float32
BF16 = jnp.bfloat16


def dotg(a, b, ca, cb):
    return lax.dot_general(a, b, (((ca,), (cb,)), ((), ())), preferred_element_type=F32)


def attend_kernel(key_block, q_ref, *refs):
    sources = refs[:-3]
    o_ref, low_ref, lse_ref = refs[-3:]
    tokens = q_ref.shape[1]
    query = q_ref[...] * BF16(SCALE)
    top = jnp.full((1, tokens), -jnp.inf, F32)
    total = jnp.zeros((1, tokens), F32)
    acc = jnp.zeros((HEAD_DIM, tokens), F32)
    for source in sources:
        for at in range(0, source.shape[1], key_block):
            ks = slice(at, at + key_block)
            scores = dotg(source[:HEAD_DIM, ks], query, 0, 0) * LOG2E
            new_top = jnp.maximum(top, jnp.max(scores, axis=0, keepdims=True))
            decay = jnp.exp2(top - new_top)
            probs = jnp.exp2(scores - new_top)
            total = total * decay + jnp.sum(probs, axis=0, keepdims=True)
            acc = acc * decay + jnp.dot(
                source[HEAD_DIM:, ks], probs.astype(BF16), preferred_element_type=F32
            )
            top = new_top
    out = acc / total
    o_ref[...] = out
    low_ref[...] = out.astype(BF16)
    lse_ref[...] = top + jnp.log2(total)


def cost(flops, nbytes):
    return pl.CostEstimate(flops=flops * 10, transcendentals=0, bytes_accessed=nbytes)


def attend(head, query, sources, key_block=1024):
    tokens = query.shape[1]
    keys = sum(s.shape[1] for s in sources)
    whole = lambda s: pl.BlockSpec(s.shape, lambda i: (0, 0))
    flat = lambda rows: pl.BlockSpec((rows, tokens), lambda i: (0, 0))
    return pl.pallas_call(
        functools.partial(attend_kernel, key_block),
        grid=(1,),
        in_specs=[pl.BlockSpec((HEAD_DIM, tokens), lambda i: (head, 0))]
        + [whole(s) for s in sources],
        out_specs=(flat(HEAD_DIM), flat(HEAD_DIM), flat(1)),
        out_shape=(
            jax.ShapeDtypeStruct((HEAD_DIM, tokens), F32),
            jax.ShapeDtypeStruct((HEAD_DIM, tokens), BF16),
            jax.ShapeDtypeStruct((1, tokens), F32),
        ),
        compiler_params=pltpu.CompilerParams(vmem_limit_bytes=60 << 20),
        cost_estimate=cost(4 * 4 * HEAD_DIM * tokens * keys, 0),
        name="attend",
    )(query, *sources)


def attend_back_kernel(key_block, n, q_ref, do_ref, o_ref, lse_ref, *refs):
    sources, dq_ref, outs = refs[:n], refs[n], refs[n + 1 :]
    query = q_ref[...] * BF16(SCALE)
    grad = do_ref[...]
    lse = lse_ref[...]
    delta = jnp.sum(grad.astype(F32) * o_ref[...], axis=0, keepdims=True)
    dq = jnp.zeros(query.shape, F32)
    tokens = sources[0].shape[1]
    for i, source in enumerate(sources):
        out, base = outs[i * len(outs) // n], i % (n // len(outs)) * tokens
        for at in range(0, tokens, key_block):
            ks = slice(at, at + key_block)
            to = slice(base + at, base + at + key_block)
            keys, values = source[:HEAD_DIM, ks], source[HEAD_DIM:, ks]
            probs = jnp.exp2(dotg(keys, query, 0, 0) * LOG2E - lse)
            gap = dotg(values, grad, 0, 0) - delta
            low = probs.astype(BF16)
            ds = (probs * gap).astype(BF16)
            out[HEAD_DIM:, to] = dotg(grad, low, 1, 1).astype(BF16)
            out[:HEAD_DIM, to] = dotg(query, ds, 1, 1).astype(BF16)
            dq = dq + jnp.dot(keys, ds, preferred_element_type=F32)
    dq_ref[...] = (dq * SCALE).astype(BF16)


def attend_back(head, query, grad, out, lse, sources, key_block=256):
    tokens = query.shape[1]
    n = len(sources)
    parts = min(n, 2)
    keys = sum(s.shape[1] for s in sources)
    whole = lambda s: pl.BlockSpec(s.shape, lambda i: (0, 0))
    mine = lambda: pl.BlockSpec((HEAD_DIM, tokens), lambda i: (head, 0))
    shapes = (jax.ShapeDtypeStruct((HEAD_DIM, tokens), BF16),) + tuple(
        jax.ShapeDtypeStruct((2 * HEAD_DIM, keys // parts), BF16) for _ in range(parts)
    )
    outs = pl.pallas_call(
        functools.partial(attend_back_kernel, key_block, n),
        grid=(1,),
        in_specs=[mine(), mine(), whole(out), whole(lse)] + [whole(s) for s in sources],
        out_specs=tuple(whole(s) for s in shapes),
        out_shape=shapes,
        compiler_params=pltpu.CompilerParams(vmem_limit_bytes=60 << 20),
        cost_estimate=cost(4 * 10 * HEAD_DIM * tokens * keys, 0),
        name="attend_back",
    )(query, grad, out, lse, *sources)
    return outs[0], list(outs[1:])


def copies(pair, parts, full, sems):
    half = parts[0].shape[0]
    made = []
    for i, part in enumerate(parts):
        at = 0 if len(parts) == 1 else pl.multiple_of((pair ^ i) * half, half)
        made.append(pltpu.make_async_copy(part, full.at[pl.ds(at, half), :], sems.at[i]))
    return made


def put_grads(parts, place_ref, terms, outs):
    for i, out in enumerate(outs):
        base = 0
        for left, right, axis in terms:
            rows, to = left.shape[axis] // parts, slice(base, base + right.shape[1])
            at = pl.multiple_of((place_ref[0] ^ i) * rows, rows) if parts > 1 else 0
            part = left[:, pl.ds(at, rows)] if axis == 1 else left[pl.ds(at, rows), :]
            value = dotg(part, right[...], 1 - axis, 0).astype(BF16)
            if parts == 1:
                out[:, to] = value
            else:
                size = out.shape[1]
                for b in range(out.shape[0]):
                    out[b ^ place_ref[2 + i], :, to] = value[b * size : (b + 1) * size, :]
            base += right.shape[1]


def middle_kernel(groups, parts, halves, chunk, place_ref, x_ref, dy_ref, gain_ref, *refs):
    pieces = refs[:groups]
    given = refs[groups : groups + 4 * parts]
    rest = refs[groups + 4 * parts :]
    out_ref, dy1_ref = rest[:2]
    back_pieces = rest[2 : 2 + groups]
    grads = rest[2 + groups : 2 + groups + 3 * halves]
    (wo, wg, wu, wd, do_ref, mixed_ref, h2_ref, hidden_ref, dgate_ref, dup_ref, da_ref) = rest[
        2 + groups + 3 * halves : 13 + groups + 3 * halves
    ]
    made_grads = rest[13 + groups + 3 * halves : 13 + groups + 6 * halves]
    sems, out_sems = rest[-2:]
    pair, group = place_ref[0], place_ref[1]
    made = [
        copies(pair, given[j * parts : (j + 1) * parts], full, sems.at[j])
        for j, full in enumerate((wo, wg, wu, wd))
    ]
    for cs in made:
        for c in cs:
            c.start()
    rows = pieces[0].shape[0]
    spot = [pl.ds(pl.multiple_of((group ^ s) * rows, rows), rows) for s in range(groups)]
    for s in range(groups):
        mixed_ref[spot[s], :] = pieces[s][...]
    for c in made[0]:
        c.wait()
    dy = dy_ref[...]
    gain = gain_ref[...].astype(F32)
    y1 = x_ref[...].astype(F32) + dotg(mixed_ref[...], wo[...], 0, 0)
    r2 = lax.rsqrt(jnp.mean(y1 * y1, axis=-1, keepdims=True) + EPS)
    h2 = (y1 * r2 * gain).astype(BF16)
    h2_ref[...] = h2
    for c in made[1] + made[2]:
        c.wait()
    result = y1
    dh2 = jnp.zeros(y1.shape, F32)
    root, cubic = math.sqrt(2 / math.pi), 0.044715
    for at in range(0, wg.shape[1], chunk):
        cs = slice(at, at + chunk)
        u = jnp.dot(h2, wg[:, cs], preferred_element_type=F32)
        upper = jnp.dot(h2, wu[:, cs], preferred_element_type=F32)
        square = u * u
        t = jnp.tanh(root * (u + cubic * (u * square)))
        share = 0.5 * (1.0 + t)
        bent = u * share
        slope = share + (0.5 * root) * u * (1.0 - t * t) * (1.0 + (3 * cubic) * square)
        hidden = (bent * upper).astype(BF16)
        hidden_ref[:, cs] = hidden
        if at == 0:
            for c in made[3]:
                c.wait()
        result = result + jnp.dot(hidden, wd[cs, :], preferred_element_type=F32)
        dhidden = dotg(dy, wd[cs, :], 1, 1)
        dgate = (dhidden * upper * slope).astype(BF16)
        dup = (dhidden * bent).astype(BF16)
        dgate_ref[:, cs] = dgate
        dup_ref[:, cs] = dup
        dh2 = dh2 + dotg(dgate, wg[:, cs], 1, 1) + dotg(dup, wu[:, cs], 1, 1)
    out_ref[...] = result.astype(BF16)
    lead = gain * dh2
    mean = jnp.mean(lead * y1, axis=-1, keepdims=True)
    dy1 = dy.astype(F32) + r2 * (lead - y1 * (r2 * r2) * mean)
    dy1_ref[...] = dy1
    da = dy1.astype(BF16)
    da_ref[...] = da
    do_ref[...] = dotg(wo[...], da, 1, 1).astype(BF16)
    for s in range(groups):
        back_pieces[s][...] = do_ref[spot[s], :]
    sent = []
    terms = (
        [(hidden_ref, dy_ref, 1)],
        [(h2_ref, dgate_ref, 1)],
        [(h2_ref, dup_ref, 1), (mixed_ref, da_ref, 0)],
    )
    for j, term in enumerate(terms):
        at = slice(j * halves, (j + 1) * halves)
        put_grads(halves, place_ref, term, made_grads[at])
        for i, (value, to) in enumerate(zip(made_grads[at], grads[at])):
            sent.append(pltpu.make_async_copy(value, to, out_sems.at[j, i]))
            sent[-1].start()
    for c in sent:
        c.wait()


def middle(place, dp, ctx, x, dy, gain, pieces, weights, ff):
    tokens, width = x.shape
    groups, parts, halves = len(pieces), len(weights[0]), 2 if dp == 2 else 1
    vmem, far = pl.BlockSpec(memory_space=pltpu.VMEM), pl.BlockSpec(memory_space=pl.ANY)
    some = lambda shape, dtype: jax.ShapeDtypeStruct(shape, dtype)

    def stack(rows, columns):
        rows //= halves
        return (ctx, rows // ctx, columns) if halves == 2 else (rows, columns)

    stacks = (stack(ff, width), stack(width, ff), stack(width, ff + width))
    stacks = [shape for shape in stacks for _ in range(halves)]
    low = lambda *shape: pltpu.VMEM(shape, BF16)
    outs = pl.pallas_call(
        functools.partial(middle_kernel, groups, parts, halves, 512),
        in_specs=[pl.BlockSpec(memory_space=pltpu.SMEM)]
        + [vmem] * (3 + groups)
        + [far] * (4 * parts),
        out_specs=(vmem,) * (2 + groups) + (far,) * len(stacks),
        out_shape=(some((tokens, width), BF16), some((tokens, width), F32))
        + tuple(some(p.shape, BF16) for p in pieces)
        + tuple(some(shape, BF16) for shape in stacks),
        scratch_shapes=[
            low(width, width),
            low(width, ff),
            low(width, ff),
            low(ff, width),
            low(width, tokens),
            low(width, tokens),
            low(tokens, width),
            low(tokens, ff),
            low(tokens, ff),
            low(tokens, ff),
            low(tokens, width),
        ]
        + [low(*shape) for shape in stacks]
        + [pltpu.SemaphoreType.DMA((4, parts)), pltpu.SemaphoreType.DMA((3, halves))],
        compiler_params=pltpu.CompilerParams(vmem_limit_bytes=60 << 20),
        cost_estimate=cost(6 * tokens * width * (width + 3 * ff), 6 * width * ff),
        name="middle",
    )(place, x, dy, gain.reshape(1, width), *pieces, *[p for w in weights for p in w])
    grads = outs[2 + groups :]
    return (
        outs[:2],
        list(outs[2 : 2 + groups]),
        [grads[j * halves : (j + 1) * halves] for j in range(3)],
    )


def ordered_kernel(n, given, code_ref, near_ref, far_ref, *refs):
    weights, outs, sums = refs[:given], refs[given : given + n], refs[given + n :]
    half, size = near_ref.shape[:2]

    def put(block, rows):
        base, total = 0, jnp.zeros((size, 1), F32)
        for i, out in enumerate(outs):
            value = block[:, base : base + out.shape[1]].astype(F32)
            out[rows, :] = value
            base += out.shape[1]
            if i < given:
                product = value * weights[i][rows, :].astype(F32)
                total = total + jnp.sum(product, axis=1, keepdims=True)
        for s in sums:
            s[rows, :] = total

    for b in range(2 * half):
        at = b ^ code_ref[2]
        rows = slice(b * size, (b + 1) * size)
        pl.when(at < half)(
            lambda at=at, rows=rows: put(near_ref[jnp.minimum(at, half - 1)], rows)
        )
        pl.when(at >= half)(
            lambda at=at, rows=rows: put(far_ref[jnp.maximum(at - half, 0)], rows)
        )


def ordered(place, near, far, columns, weights=()):
    rows = 2 * near.shape[0] * near.shape[1]
    vmem = pl.BlockSpec(memory_space=pltpu.VMEM)
    shapes = [jax.ShapeDtypeStruct((rows, c), F32) for c in columns]
    shapes += [jax.ShapeDtypeStruct((rows, 1), F32)] * min(len(weights), 1)
    return pl.pallas_call(
        functools.partial(ordered_kernel, len(columns), len(weights)),
        in_specs=[pl.BlockSpec(memory_space=pltpu.SMEM)] + [vmem] * (2 + len(weights)),
        out_specs=(vmem,) * len(shapes),
        out_shape=tuple(shapes),
        compiler_params=pltpu.CompilerParams(vmem_limit_bytes=60 << 20),
        cost_estimate=cost(near.size, 0),
        name="ordered",
    )(place, near, far, *weights)


def head_grads_kernel(heads, devices, parts, place_ref, *refs):
    outs = refs[-parts:]
    queries, pairs = refs[:heads], refs[heads : 2 * heads]
    rows = refs[2 * heads : -parts]
    d = jnp.concatenate(
        [q[...] for q in queries]
        + [p[:HEAD_DIM, :] for p in pairs]
        + [p[HEAD_DIM:, :] for p in pairs],
        axis=0,
    )
    width = rows[0].shape[1] // parts
    for i, out in enumerate(outs):
        at = pl.multiple_of((place_ref[0] ^ i) * width, width) if parts > 1 else 0
        left = jnp.concatenate([r[:, pl.ds(at, width)] for r in rows], axis=0)
        out[...] = jnp.dot(d, left, preferred_element_type=F32).T.astype(BF16)


def head_grads(place, dp, queries, pairs, rows):
    heads, parts = len(queries), 2 if dp == 2 else 1
    width, columns = rows[0].shape[1], 3 * HEAD_DIM * heads
    vmem = pl.BlockSpec(memory_space=pltpu.VMEM)
    return pl.pallas_call(
        functools.partial(head_grads_kernel, heads, dp, parts),
        in_specs=[pl.BlockSpec(memory_space=pltpu.SMEM)] + [vmem] * (2 * heads + len(rows)),
        out_specs=(vmem,) * parts,
        out_shape=(jax.ShapeDtypeStruct((width // parts, columns), BF16),) * parts,
        compiler_params=pltpu.CompilerParams(vmem_limit_bytes=60 << 20),
        cost_estimate=cost(2 * queries[0].shape[1] * width * columns, 0),
        name="head_grads",
    )(place, *queries, *pairs, *rows)


def unstacked(value, base, rows, cols):
    n = cols // LANES
    part = value[base : base + rows * n].reshape(n, rows, LANES)
    return part.transpose(1, 0, 2).reshape(rows, cols).astype(F32)


class Plan:
    def __init__(self, dp, ctx):
        self.dp, self.ctx = dp, ctx
        self.groups = math.gcd(HEADS, ctx)
        self.rest = ctx // self.groups
        self.bits = self.rest.bit_length() - 1
        self.group_bits = self.groups.bit_length() - 1
        assert 1 << self.bits == self.rest and self.groups & (self.groups - 1) == 0

    def bit(self, parity, step):
        return step if parity == 0 else self.bits - 1 - step

    def rest_perm(self, step):
        return [
            (d * self.ctx + c, d * self.ctx + (c ^ (1 << self.bit(d % 2, step))))
            for d in range(self.dp)
            for c in range(self.ctx)
        ]

    def group_perm(self, s):
        return [(c, c ^ (s * self.rest)) for c in range(self.ctx)]

    def group(self):
        return lax.axis_index("ctx") // self.rest

    def my_bit(self, step, other=0):
        c = lax.axis_index("ctx")
        even = (c >> self.bit(0, step)) & 1
        odd = (c >> self.bit(1, step)) & 1
        return jnp.where((lax.axis_index("dp") + other) % 2 == 0, even, odd)

    def over_rest(self, value, step):
        return lax.ppermute(value, AXES, self.rest_perm(step))

    def over_group(self, value, s):
        return value if s == 0 else lax.ppermute(value, "ctx", self.group_perm(s))

    def gather_rest(self, value):
        blocks = [value]
        for step in range(self.bits):
            came = yield [
                (b, lambda v, step=step: self.over_rest(v, step)) for b in blocks
            ]
            blocks = blocks + came
        return blocks

    def natural(self, pieces, axis=0):
        g = self.group()
        step = 1
        while step < self.groups:
            odd = (g & step) != 0
            pieces = [
                jnp.where(odd, pieces[i ^ step], pieces[i]) for i in range(self.groups)
            ]
            step *= 2
        return jnp.concatenate(pieces, axis=axis)

    def hop(self, step):
        if step < self.bits:
            return lambda v: self.over_rest(v, step)
        return lambda v: self.over_group(v, 1 << (step - self.bits))

    def place_bit(self, step, other=0):
        if step < self.bits:
            return self.my_bit(step, other)
        return (self.group() >> (step - self.bits)) & 1

    def halves(self, value, step):
        half = value.shape[0] // 2
        b = self.place_bit(step)
        return (
            lax.dynamic_slice_in_dim(value, b * half, half, 0),
            lax.dynamic_slice_in_dim(value, (1 - b) * half, half, 0),
        )

    def group_pieces(self, value):
        size = value.shape[0] // self.groups
        return [
            lax.dynamic_slice_in_dim(value, (self.group() ^ s) * size, size, 0)
            for s in range(self.groups)
        ]

    def to_rest(self, value, step):
        return [(value, lambda v: self.over_rest(v, step))]

    def to_groups(self, pieces):
        return [
            (p, lambda v, s=s: self.over_group(v, s)) for s, p in enumerate(pieces) if s
        ]

    def exchange(self, pieces):
        came = yield self.to_groups(pieces)
        return [pieces[0]] + came

    def send_group(self, value, s):
        came = yield [(value, lambda v: self.over_group(v, s))]
        return came[0]

    def scatter_rest(self, parts):
        for step in reversed(range(self.bits)):
            if step < self.bits - 1:
                half = parts.shape[1] // 2
                parts = parts[:, :half], parts[:, half:]
            came = yield self.to_rest(parts[1], step)
            parts = add_low(parts[0], came[0])
        return parts if self.bits else parts[0]

    def reduce_rows(self, value, steps):
        for step in range(steps):
            kept, gone = self.halves(value, step)
            came = yield [(gone, self.hop(step))]
            value = add_low(kept, came[0])
        return value

    def expand_rows(self, value, steps):
        for step in reversed(range(steps)):
            came = yield [(value, self.hop(step))]
            value = jnp.where(
                self.place_bit(step) == 0,
                jnp.concatenate([value, came[0]], axis=0),
                jnp.concatenate([came[0], value], axis=0),
            )
        return value

    def code(self, other):
        steps = self.bits + self.group_bits
        total = 0
        for step in range(steps):
            total = total + (self.place_bit(step, other) << (steps - 1 - step))
        return total

    def sum_blocks(self, pair, stacks):
        steps = self.bits + self.group_bits
        terms = yield from pair.combine(stacks)
        for step in range(steps):
            half = terms[0].shape[0] // 2
            came = yield [(total_low([t[half:] for t in terms]), self.hop(step))]
            terms = [t[:half] for t in terms] + came
        value = total_low(terms)
        for step in reversed(range(steps)):
            came = yield [(value, self.hop(step))]
            halves = [value] + came
            value = jnp.concatenate(halves, axis=0) if step else halves
        return value

    def sum_rows(self, pair, stacks):
        terms = yield from pair.combine(stacks)
        value = yield from self.reduce_rows(total_low(terms), self.bits + self.group_bits)
        return (yield from self.expand_rows(value, self.bits + self.group_bits))

    def sum_heads(self, pair, stacks, columns):
        terms = yield from pair.combine(stacks)
        value = yield from self.reduce_rows(total_low(terms), self.bits)
        rows, groups = value.shape[0], [value]
        for step in range(self.group_bits):
            came = yield [(jnp.concatenate(groups, axis=0), self.hop(self.bits + step))]
            groups = groups + [
                came[0][i * rows : (i + 1) * rows] for i in range(len(groups))
            ]
        value = jnp.concatenate(
            [
                self.natural([p[:, at : at + columns] for p in groups], 1)
                for at in range(0, value.shape[1], columns)
            ],
            axis=1,
        )
        return (yield from self.expand_rows(value, self.bits))


def add_low(a, b):
    return (a.astype(F32) + b.astype(F32)).astype(BF16)


def total_low(terms):
    return functools.reduce(jnp.add, [t.astype(F32) for t in terms]).astype(BF16)


class Chain:
    def __init__(self, name, stages):
        self.name, self.stages, self.came, self.result = name, stages, None, None
        self.stage = 0

    def send(self, moves, values):
        self.stage += 1
        with jax.named_scope(f"{self.name}_{self.stage}"):
            self.came = [move(v) for v, (_, move) in zip(values, moves)]

    def next_moves(self):
        if self.result is not None:
            return []
        try:
            return self.stages.send(self.came)
        except StopIteration as end:
            self.came, self.result = None, end.value
            return []


class Order:
    def __init__(self, token):
        self.token = token

    def __call__(self, land, launch, values=()):
        moves = [c.next_moves() for c in launch]
        waiting = [c for c in land if c not in launch and c.came is not None]
        ended = [c for c in launch if c.result is not None]
        self.token, values, held, done, sent = lax.optimization_barrier(
            (
                self.token,
                values,
                [c.came for c in waiting],
                [c.result for c in ended],
                [[v for v, _ in m] for m in moves],
            )
        )
        for c, came in zip(waiting, held):
            c.came = came
        for c, result in zip(ended, done):
            c.result = result
        for c, m, vs in zip(launch, moves, sent):
            if m:
                c.send(m, vs)
        return values


def finish(*chains):
    while any(c.result is None for c in chains):
        for c in chains:
            m = c.next_moves()
            if m:
                c.send(m, [v for v, _ in m])
    return [c.result for c in chains]


def add_low(a, b):
    return (a.astype(F32) + b.astype(F32)).astype(BF16)


def total_low(terms):
    return functools.reduce(jnp.add, [t.astype(F32) for t in terms]).astype(BF16)


class Pair:
    def __init__(self, dp):
        self.dp = dp
        self.me = lax.axis_index("dp")

    def swap(self, value):
        return lax.ppermute(value, "dp", [(0, 1), (1, 0)])

    def gather(self, weight):
        if self.dp != 2:
            return [lax.all_gather(weight, "dp", axis=0, tiled=True)]
        came = yield [(weight, self.swap)]
        return [weight] + came

    def part(self, value, i, axis):
        if self.dp != 2:
            return value
        half = value.shape[axis] // 2
        at = jnp.where(self.me == i, 0, half)
        return lax.dynamic_slice_in_dim(value, at, half, axis)

    def join(self, parts, axis):
        if len(parts) == 1:
            return parts[0]
        return jnp.where(
            self.me == 0,
            jnp.concatenate(parts, axis),
            jnp.concatenate(parts[::-1], axis),
        )

    def times(self, value, axis, weight, contract):
        return functools.reduce(
            jnp.add,
            [
                contract(self.part(value, i, axis), w)
                for i, w in enumerate(weight)
            ],
        )

    def combine(self, stacks):
        if self.dp == 2:
            came = yield [(stacks[1], self.swap)]
            return [stacks[0]] + came
        return [lax.psum_scatter(stacks[0], "dp", scatter_dimension=0, tiled=True)]


def scaled(rows):
    return lax.rsqrt(jnp.mean(rows * rows, axis=-1, keepdims=True) + EPS)


def norm_back(rows, r, gain, grad):
    lead = gain * grad
    return r * (lead - rows * (r * r) * jnp.mean(lead * rows, axis=-1, keepdims=True))


def gain_grad(gain, *pairs):
    total = sum(jnp.sum(w.astype(F32) * g, axis=1) for w, g in pairs)
    return total / gain.astype(F32)


def on_device(
    dp,
    ctx,
    layer_in,
    out_grad,
    first_gain,
    query_weight,
    key_weight,
    value_weight,
    output_weight,
    second_gain,
    gate_weight,
    up_weight,
    down_weight,
):
    plan, pair = Plan(dp, ctx), Pair(dp)
    _, local, width = layer_in.shape
    ff = gate_weight.shape[1]
    heads, group_width = HEADS // plan.groups, width // plan.groups
    place = jnp.stack([pair.me, plan.group(), plan.code(0), plan.code(1)]).astype(jnp.int32)

    gains_given = jnp.stack([first_gain, second_gain], 1)
    gains_full, w_key, w_value, w_query = finish(
        *[
            Chain("weights", pair.gather(w))
            for w in (gains_given, key_weight, value_weight, query_weight)
        ]
    )
    gains_full = pair.join(gains_full, 0)
    gain_one = gains_full[:, 0].astype(F32)
    x = layer_in.reshape(local, width).astype(F32)
    r1 = scaled(x)
    h1 = (x * r1 * gain_one).astype(BF16)

    def project(w):
        return pair.times(h1, 1, w, lambda a, b: dotg(b, a, 0, 1)).astype(BF16)

    keys, values, query = project(w_key), project(w_value), project(w_query)

    def by_token(value):
        return [value[:, i * local : (i + 1) * local] for i in range(plan.groups)]

    paired = jnp.concatenate(
        [a.reshape(HEADS, HEAD_DIM, local) for a in (keys, values)], axis=1
    ).reshape(2 * width, local)
    order = Order(place)
    kv = Chain("kv", plan.exchange(plan.group_pieces(paired)))
    qs = Chain("qs", plan.exchange(plan.group_pieces(query)))
    later = [
        Chain("weights", pair.gather(w))
        for w in (output_weight, gate_weight, up_weight, down_weight)
    ]
    order([], [kv])
    order([], later[:2])
    order(later[:2], later[2:])
    order(later[2:] + [kv], [qs])
    weights = finish(*later)
    kv = jnp.concatenate(finish(kv)[0], axis=1)
    gather = [
        Chain("keys", plan.gather_rest(kv[2 * HEAD_DIM * h : 2 * HEAD_DIM * (h + 1)]))
        for h in range(heads)
    ]
    spread = [Chain("spread", plan.send_group(h1, i)) for i in range(1, plan.groups)]
    order([], gather[:2])
    for step in range(1, plan.bits):
        order(gather[:1], gather[:1])
    q = jnp.concatenate(finish(qs)[0], axis=1)
    outs = []
    for h in range(heads):
        (sources,) = finish(gather[h])
        coming = gather[h + 1 : h + 2] if plan.bits > 1 else []
        near = spread[:2] if h == 0 else spread[2:] if h == 2 else []
        q, sources, outs = order(
            coming + (spread[h - 1 : h] if h else []), coming + gather[h + 2 : h + 3] + near, (q, sources, outs)
        )
        gather[h].result = sources
        outs = outs + [attend(h, q, sources)]
    o_wide, o_low, lse = zip(*outs)
    sources = [c.result for c in gather]
    mixed = Chain("mixed", plan.exchange(by_token(jnp.concatenate(o_low, axis=0))))
    order([], [mixed])
    order(spread, [mixed])
    mixed = mixed.result
    dy = out_grad.reshape(local, width)
    (layer_out, dy1), do_pieces, made = middle(
        place, dp, ctx, layer_in.reshape(local, width), dy, gains_full[:, 1], mixed, weights, ff
    )
    d_mixed = [
        Chain("d_mixed", plan.send_group(p, s)) for s, p in enumerate(do_pieces) if s
    ]
    order([], d_mixed)
    back = lambda h, do: attend_back(h, q, do, o_wide[h], lse[h], sources[h])

    def sums(stacks):
        return plan.sum_blocks(pair, stacks) if dp == 2 else plan.sum_rows(pair, stacks)

    downs = Chain("downs", sums(made[0]))
    gates = Chain("gates", sums(made[1]))
    ups = Chain("ups", sums(made[2]))
    order([], [downs])
    order([downs], [downs])
    order([], [gates])
    order(d_mixed, [])
    order([], [ups])
    do = jnp.concatenate(do_pieces[:1] + finish(*d_mixed), axis=1)
    do = order([downs, gates], [downs, gates], do)
    dq0, pair0 = back(0, do)
    k0 = Chain("k0", plan.scatter_rest(pair0))
    do, dq0 = order([gates, downs, ups], [ups, gates, downs], (do, dq0))
    dq1, pair1 = back(1, do)
    k1 = Chain("k1", plan.scatter_rest(pair1))
    do, dq1 = order([gates, downs], [gates, downs, k0], (do, dq1))
    dq2, pair2 = back(2, do)
    k2 = Chain("k2", plan.scatter_rest(pair2))
    dq2 = order([k0, gates, downs, ups], [ups, k1, k0, gates, downs], dq2)
    order([k0, downs], [k2, downs])
    order([k1, gates], [k1, gates])
    order([k2, ups], [k2, ups])
    pair0, pair1, pair2 = finish(k0, k1, k2)
    rows = [h1] + finish(*spread)
    third = Chain(
        "third",
        plan.sum_heads(
            pair,
            head_grads(place, dp, (dq0, dq1, dq2), (pair0, pair1, pair2), rows),
            heads * HEAD_DIM,
        ),
    )
    d_all = Chain(
        "d_all",
        plan.exchange(
            by_token(jnp.concatenate([dq0, dq1, dq2, pair0, pair1, pair2], axis=0))
        ),
    )
    order([], [third])
    order([third, gates, downs], [third, gates, downs])
    order([ups], [ups])
    order([third], [third])
    order([gates, downs], [gates, downs])
    order([ups], [ups])
    order([third], [third])
    order([gates], [gates])
    order([ups], [ups])
    order([third], [third])
    order([ups], [ups])
    order([], [d_all])
    order([third], [third])
    order([ups], [ups])
    order([third], [third])
    order([d_all], [])
    d_all = plan.natural(finish(d_all)[0]).reshape(plan.groups, 3 * heads, HEAD_DIM, local)
    pick = lambda at: jnp.stack([d_all[:, i] for i in at], 1).reshape(width, local)
    d_query = pick(range(heads))
    d_key = pick(range(heads, 3 * heads, 2))
    d_value = pick(range(heads + 1, 3 * heads, 2))
    dh1 = pair.join(
        [
            dotg(d_query, a, 0, 1) + dotg(d_key, b, 0, 1) + dotg(d_value, c, 0, 1)
            for a, b, c in zip(w_query, w_key, w_value)
        ],
        1,
    )
    back_one = norm_back(x, r1, gain_one, dh1)
    in_grad = (back_one + dy1).astype(BF16).reshape(layer_in.shape)

    (third,) = finish(third)
    third = third.astype(F32)
    d_wq, d_wk, d_wv = (third[:, i * width : (i + 1) * width] for i in range(3))
    gain_one_grad = gain_grad(
        first_gain, (query_weight, d_wq), (key_weight, d_wk), (value_weight, d_wv)
    )
    downs, gates = finish(downs, gates)
    if dp == 2:
        (downs,) = ordered(place, *downs, [width])
        d_gate, total = ordered(place, *gates, [ff], (gate_weight,))
    else:
        downs, d_gate = downs.astype(F32), gates.astype(F32)
    early = (in_grad, downs, d_gate, d_wq, d_wk, d_wv, gain_one_grad)
    in_grad, downs, d_gate, d_wq, d_wk, d_wv, gain_one_grad = order([], [], early)
    order([ups], [])
    place = order.token
    (ups,) = finish(ups)
    if dp == 2:
        d_up, d_wo, rest = ordered(place, *ups, [ff, width], (up_weight,))
        gain_two_grad = (total + rest)[:, 0] / second_gain.astype(F32)
    else:
        ups = ups.astype(F32)
        d_up, d_wo = ups[:, :ff], ups[:, ff:]
        gain_two_grad = gain_grad(second_gain, (gate_weight, d_gate), (up_weight, d_up))
    return (
        layer_out.reshape(layer_in.shape),
        in_grad,
        gain_one_grad,
        d_wq,
        d_wk,
        d_wv,
        d_wo,
        gain_two_grad,
        d_gate,
        d_up,
        downs,
    )


def solution(mesh):
    tokens, matrix, vector = P("dp", "ctx", None), P("dp", None), P("dp")
    weights = (vector, matrix, matrix, matrix, matrix, vector, matrix, matrix, matrix)
    return jax.shard_map(
        functools.partial(on_device, mesh.shape["dp"], mesh.shape["ctx"]),
        mesh=mesh,
        in_specs=(tokens, tokens) + weights,
        out_specs=(tokens, tokens) + weights,
        check_vma=False,
    )
```

```python
import functools
import math

import jax
import jax.numpy as jnp
from jax import lax
from jax.experimental import pallas as pl
from jax.experimental.pallas import tpu as pltpu
from jax.sharding import PartitionSpec as P

HEADS = 12
HEAD_DIM = 64
EPS = 1e-06
LOG2E = 1.4426950408889634
SCALE = HEAD_DIM ** (-0.5)
AXES = ("dp", "ctx")
F32 = jnp.float32
BF16 = jnp.bfloat16


def dotg(a, b, ca, cb):
    return lax.dot_general(a, b, (((ca,), (cb,)), ((), ())), preferred_element_type=F32)


def attend_kernel(key_block, q_ref, *refs):
    sources = refs[:-3]
    o_ref, low_ref, lse_ref = refs[-3:]
    tokens = q_ref.shape[1]
    query = q_ref[...] * BF16(SCALE)
    top = jnp.full((1, tokens), -jnp.inf, F32)
    total = jnp.zeros((1, tokens), F32)
    acc = jnp.zeros((HEAD_DIM, tokens), F32)
    for source in sources:
        for at in range(0, source.shape[1], key_block):
            ks = slice(at, at + key_block)
            scores = dotg(source[:HEAD_DIM, ks], query, 0, 0) * LOG2E
            new_top = jnp.maximum(top, jnp.max(scores, axis=0, keepdims=True))
            decay = jnp.exp2(top - new_top)
            probs = jnp.exp2(scores - new_top)
            total = total * decay + jnp.sum(probs, axis=0, keepdims=True)
            acc = acc * decay + jnp.dot(
                source[HEAD_DIM:, ks], probs.astype(BF16), preferred_element_type=F32
            )
            top = new_top
    out = acc / total
    o_ref[...] = out
    low_ref[...] = out.astype(BF16)
    lse_ref[...] = top + jnp.log2(total)


def cost(flops, nbytes):
    return pl.CostEstimate(flops=flops * 3, transcendentals=0, bytes_accessed=nbytes)


def attend(head, query, sources, key_block=1024):
    tokens = query.shape[1]
    keys = sum(s.shape[1] for s in sources)
    whole = lambda s: pl.BlockSpec(s.shape, lambda i: (0, 0))
    flat = lambda rows: pl.BlockSpec((rows, tokens), lambda i: (0, 0))
    return pl.pallas_call(
        functools.partial(attend_kernel, key_block),
        grid=(1,),
        in_specs=[pl.BlockSpec((HEAD_DIM, tokens), lambda i: (head, 0))]
        + [whole(s) for s in sources],
        out_specs=(flat(HEAD_DIM), flat(HEAD_DIM), flat(1)),
        out_shape=(
            jax.ShapeDtypeStruct((HEAD_DIM, tokens), F32),
            jax.ShapeDtypeStruct((HEAD_DIM, tokens), BF16),
            jax.ShapeDtypeStruct((1, tokens), F32),
        ),
        compiler_params=pltpu.CompilerParams(vmem_limit_bytes=60 << 20),
        cost_estimate=cost(4 * 4 * HEAD_DIM * tokens * keys, 0),
        name="attend",
    )(query, *sources)


def attend_back_kernel(key_block, n, q_ref, do_ref, o_ref, lse_ref, *refs):
    sources, dq_ref, outs = refs[:n], refs[n], refs[n + 1 :]
    query = q_ref[...] * BF16(SCALE)
    grad = do_ref[...]
    lse = lse_ref[...]
    delta = jnp.sum(grad.astype(F32) * o_ref[...], axis=0, keepdims=True)
    dq = jnp.zeros(query.shape, F32)
    tokens = sources[0].shape[1]
    for i, source in enumerate(sources):
        out, base = outs[i * len(outs) // n], i % (n // len(outs)) * tokens
        for at in range(0, tokens, key_block):
            ks = slice(at, at + key_block)
            to = slice(base + at, base + at + key_block)
            keys, values = source[:HEAD_DIM, ks], source[HEAD_DIM:, ks]
            probs = jnp.exp2(dotg(keys, query, 0, 0) * LOG2E - lse)
            gap = dotg(values, grad, 0, 0) - delta
            low = probs.astype(BF16)
            ds = (probs * gap).astype(BF16)
            out[HEAD_DIM:, to] = dotg(grad, low, 1, 1).astype(BF16)
            out[:HEAD_DIM, to] = dotg(query, ds, 1, 1).astype(BF16)
            dq = dq + jnp.dot(keys, ds, preferred_element_type=F32)
    dq_ref[...] = (dq * SCALE).astype(BF16)


def attend_back(head, query, grad, out, lse, sources, key_block=256):
    tokens = query.shape[1]
    n = len(sources)
    parts = min(n, 2)
    keys = sum(s.shape[1] for s in sources)
    whole = lambda s: pl.BlockSpec(s.shape, lambda i: (0, 0))
    mine = lambda: pl.BlockSpec((HEAD_DIM, tokens), lambda i: (head, 0))
    shapes = (jax.ShapeDtypeStruct((HEAD_DIM, tokens), BF16),) + tuple(
        jax.ShapeDtypeStruct((2 * HEAD_DIM, keys // parts), BF16) for _ in range(parts)
    )
    outs = pl.pallas_call(
        functools.partial(attend_back_kernel, key_block, n),
        grid=(1,),
        in_specs=[mine(), mine(), whole(out), whole(lse)] + [whole(s) for s in sources],
        out_specs=tuple(whole(s) for s in shapes),
        out_shape=shapes,
        compiler_params=pltpu.CompilerParams(vmem_limit_bytes=60 << 20),
        cost_estimate=cost(4 * 10 * HEAD_DIM * tokens * keys, 0),
        name="attend_back",
    )(query, grad, out, lse, *sources)
    return outs[0], list(outs[1:])


def copies(pair, parts, full, sems):
    half = parts[0].shape[0]
    made = []
    for i, part in enumerate(parts):
        at = 0 if len(parts) == 1 else pl.multiple_of((pair ^ i) * half, half)
        made.append(pltpu.make_async_copy(part, full.at[pl.ds(at, half), :], sems.at[i]))
    return made


def put_grads(parts, place_ref, terms, outs):
    for i, out in enumerate(outs):
        base = 0
        for left, right, axis in terms:
            rows, to = left.shape[axis] // parts, slice(base, base + right.shape[1])
            at = pl.multiple_of((place_ref[0] ^ i) * rows, rows) if parts > 1 else 0
            part = left[:, pl.ds(at, rows)] if axis == 1 else left[pl.ds(at, rows), :]
            value = dotg(part, right[...], 1 - axis, 0).astype(BF16)
            if parts == 1:
                out[:, to] = value
            else:
                size = out.shape[1]
                for b in range(out.shape[0]):
                    out[b ^ place_ref[2 + i], :, to] = value[b * size : (b + 1) * size, :]
            base += right.shape[1]


def middle_kernel(groups, parts, halves, chunk, place_ref, x_ref, dy_ref, gain_ref, *refs):
    pieces = refs[:groups]
    given = refs[groups : groups + 4 * parts]
    rest = refs[groups + 4 * parts :]
    out_ref, dy1_ref = rest[:2]
    back_pieces = rest[2 : 2 + groups]
    grads = rest[2 + groups : 2 + groups + 3 * halves]
    (wo, wg, wu, wd, do_ref, mixed_ref, h2_ref, hidden_ref, dgate_ref, dup_ref, da_ref) = rest[
        2 + groups + 3 * halves : 13 + groups + 3 * halves
    ]
    made_grads = rest[13 + groups + 3 * halves : 13 + groups + 6 * halves]
    sems, out_sems = rest[-2:]
    pair, group = place_ref[0], place_ref[1]
    made = [
        copies(pair, given[j * parts : (j + 1) * parts], full, sems.at[j])
        for j, full in enumerate((wo, wg, wu, wd))
    ]
    for cs in made:
        for c in cs:
            c.start()
    rows = pieces[0].shape[0]
    spot = [pl.ds(pl.multiple_of((group ^ s) * rows, rows), rows) for s in range(groups)]
    for s in range(groups):
        mixed_ref[spot[s], :] = pieces[s][...]
    for c in made[0]:
        c.wait()
    dy = dy_ref[...]
    gain = gain_ref[...].astype(F32)
    y1 = x_ref[...].astype(F32) + dotg(mixed_ref[...], wo[...], 0, 0)
    r2 = lax.rsqrt(jnp.mean(y1 * y1, axis=-1, keepdims=True) + EPS)
    h2 = (y1 * r2 * gain).astype(BF16)
    h2_ref[...] = h2
    for c in made[1] + made[2]:
        c.wait()
    result = y1
    dh2 = jnp.zeros(y1.shape, F32)
    root, cubic = math.sqrt(2 / math.pi), 0.044715
    for at in range(0, wg.shape[1], chunk):
        cs = slice(at, at + chunk)
        u = jnp.dot(h2, wg[:, cs], preferred_element_type=F32)
        upper = jnp.dot(h2, wu[:, cs], preferred_element_type=F32)
        square = u * u
        t = jnp.tanh(root * (u + cubic * (u * square)))
        share = 0.5 * (1.0 + t)
        bent = u * share
        slope = share + (0.5 * root) * u * (1.0 - t * t) * (1.0 + (3 * cubic) * square)
        hidden = (bent * upper).astype(BF16)
        hidden_ref[:, cs] = hidden
        if at == 0:
            for c in made[3]:
                c.wait()
        result = result + jnp.dot(hidden, wd[cs, :], preferred_element_type=F32)
        dhidden = dotg(dy, wd[cs, :], 1, 1)
        dgate = (dhidden * upper * slope).astype(BF16)
        dup = (dhidden * bent).astype(BF16)
        dgate_ref[:, cs] = dgate
        dup_ref[:, cs] = dup
        dh2 = dh2 + dotg(dgate, wg[:, cs], 1, 1) + dotg(dup, wu[:, cs], 1, 1)
    out_ref[...] = result.astype(BF16)
    lead = gain * dh2
    mean = jnp.mean(lead * y1, axis=-1, keepdims=True)
    dy1 = dy.astype(F32) + r2 * (lead - y1 * (r2 * r2) * mean)
    dy1_ref[...] = dy1
    da = dy1.astype(BF16)
    da_ref[...] = da
    do_ref[...] = dotg(wo[...], da, 1, 1).astype(BF16)
    for s in range(groups):
        back_pieces[s][...] = do_ref[spot[s], :]
    sent = []
    terms = (
        [(hidden_ref, dy_ref, 1)],
        [(h2_ref, dgate_ref, 1)],
        [(h2_ref, dup_ref, 1), (mixed_ref, da_ref, 0)],
    )
    for j, term in enumerate(terms):
        at = slice(j * halves, (j + 1) * halves)
        put_grads(halves, place_ref, term, made_grads[at])
        for i, (value, to) in enumerate(zip(made_grads[at], grads[at])):
            sent.append(pltpu.make_async_copy(value, to, out_sems.at[j, i]))
            sent[-1].start()
    for c in sent:
        c.wait()


def middle(place, dp, ctx, x, dy, gain, pieces, weights, ff):
    tokens, width = x.shape
    groups, parts, halves = len(pieces), len(weights[0]), 2 if dp == 2 else 1
    vmem, far = pl.BlockSpec(memory_space=pltpu.VMEM), pl.BlockSpec(memory_space=pl.ANY)
    some = lambda shape, dtype: jax.ShapeDtypeStruct(shape, dtype)

    def stack(rows, columns):
        rows //= halves
        return (ctx, rows // ctx, columns) if halves == 2 else (rows, columns)

    stacks = (stack(ff, width), stack(width, ff), stack(width, ff + width))
    stacks = [shape for shape in stacks for _ in range(halves)]
    low = lambda *shape: pltpu.VMEM(shape, BF16)
    outs = pl.pallas_call(
        functools.partial(middle_kernel, groups, parts, halves, 512),
        in_specs=[pl.BlockSpec(memory_space=pltpu.SMEM)]
        + [vmem] * (3 + groups)
        + [far] * (4 * parts),
        out_specs=(vmem,) * (2 + groups) + (far,) * len(stacks),
        out_shape=(some((tokens, width), BF16), some((tokens, width), F32))
        + tuple(some(p.shape, BF16) for p in pieces)
        + tuple(some(shape, BF16) for shape in stacks),
        scratch_shapes=[
            low(width, width),
            low(width, ff),
            low(width, ff),
            low(ff, width),
            low(width, tokens),
            low(width, tokens),
            low(tokens, width),
            low(tokens, ff),
            low(tokens, ff),
            low(tokens, ff),
            low(tokens, width),
        ]
        + [low(*shape) for shape in stacks]
        + [pltpu.SemaphoreType.DMA((4, parts)), pltpu.SemaphoreType.DMA((3, halves))],
        compiler_params=pltpu.CompilerParams(vmem_limit_bytes=60 << 20),
        cost_estimate=cost(6 * tokens * width * (width + 3 * ff), 6 * width * ff),
        name="middle",
    )(place, x, dy, gain.reshape(1, width), *pieces, *[p for w in weights for p in w])
    grads = outs[2 + groups :]
    return (
        outs[:2],
        list(outs[2 : 2 + groups]),
        [grads[j * halves : (j + 1) * halves] for j in range(3)],
    )


def ordered_kernel(n, given, code_ref, near_ref, far_ref, *refs):
    weights, outs, sums = refs[:given], refs[given : given + n], refs[given + n :]
    half, size = near_ref.shape[:2]

    def put(block, rows):
        base, total = 0, jnp.zeros((size, 1), F32)
        for i, out in enumerate(outs):
            value = block[:, base : base + out.shape[1]].astype(F32)
            out[rows, :] = value
            base += out.shape[1]
            if i < given:
                product = value * weights[i][rows, :].astype(F32)
                total = total + jnp.sum(product, axis=1, keepdims=True)
        for s in sums:
            s[rows, :] = total

    for b in range(2 * half):
        at = b ^ code_ref[2]
        rows = slice(b * size, (b + 1) * size)
        pl.when(at < half)(
            lambda at=at, rows=rows: put(near_ref[jnp.minimum(at, half - 1)], rows)
        )
        pl.when(at >= half)(
            lambda at=at, rows=rows: put(far_ref[jnp.maximum(at - half, 0)], rows)
        )


def ordered(place, near, far, columns, weights=()):
    rows = 2 * near.shape[0] * near.shape[1]
    vmem = pl.BlockSpec(memory_space=pltpu.VMEM)
    shapes = [jax.ShapeDtypeStruct((rows, c), F32) for c in columns]
    shapes += [jax.ShapeDtypeStruct((rows, 1), F32)] * min(len(weights), 1)
    return pl.pallas_call(
        functools.partial(ordered_kernel, len(columns), len(weights)),
        in_specs=[pl.BlockSpec(memory_space=pltpu.SMEM)] + [vmem] * (2 + len(weights)),
        out_specs=(vmem,) * len(shapes),
        out_shape=tuple(shapes),
        compiler_params=pltpu.CompilerParams(vmem_limit_bytes=60 << 20),
        cost_estimate=cost(near.size, 0),
        name="ordered",
    )(place, near, far, *weights)


def head_grads_kernel(heads, devices, parts, place_ref, *refs):
    outs = refs[-parts:]
    queries, pairs = refs[:heads], refs[heads : 2 * heads]
    rows = refs[2 * heads : -parts]
    d = jnp.concatenate(
        [q[...] for q in queries]
        + [p[:HEAD_DIM, :] for p in pairs]
        + [p[HEAD_DIM:, :] for p in pairs],
        axis=0,
    )
    width = rows[0].shape[1] // parts
    for i, out in enumerate(outs):
        at = pl.multiple_of((place_ref[0] ^ i) * width, width) if parts > 1 else 0
        left = jnp.concatenate([r[:, pl.ds(at, width)] for r in rows], axis=0)
        out[...] = jnp.dot(d, left, preferred_element_type=F32).T.astype(BF16)


def head_grads(place, dp, queries, pairs, rows):
    heads, parts = len(queries), 2 if dp == 2 else 1
    width, columns = rows[0].shape[1], 3 * HEAD_DIM * heads
    vmem = pl.BlockSpec(memory_space=pltpu.VMEM)
    return pl.pallas_call(
        functools.partial(head_grads_kernel, heads, dp, parts),
        in_specs=[pl.BlockSpec(memory_space=pltpu.SMEM)] + [vmem] * (2 * heads + len(rows)),
        out_specs=(vmem,) * parts,
        out_shape=(jax.ShapeDtypeStruct((width // parts, columns), BF16),) * parts,
        compiler_params=pltpu.CompilerParams(vmem_limit_bytes=60 << 20),
        cost_estimate=cost(2 * queries[0].shape[1] * width * columns, 0),
        name="head_grads",
    )(place, *queries, *pairs, *rows)


def unstacked(value, base, rows, cols):
    n = cols // LANES
    part = value[base : base + rows * n].reshape(n, rows, LANES)
    return part.transpose(1, 0, 2).reshape(rows, cols).astype(F32)


class Plan:
    def __init__(self, dp, ctx):
        self.dp, self.ctx = dp, ctx
        self.groups = math.gcd(HEADS, ctx)
        self.rest = ctx // self.groups
        self.bits = self.rest.bit_length() - 1
        self.group_bits = self.groups.bit_length() - 1
        assert 1 << self.bits == self.rest and self.groups & (self.groups - 1) == 0

    def bit(self, parity, step):
        return step if parity == 0 else self.bits - 1 - step

    def rest_perm(self, step):
        return [
            (d * self.ctx + c, d * self.ctx + (c ^ (1 << self.bit(d % 2, step))))
            for d in range(self.dp)
            for c in range(self.ctx)
        ]

    def group_perm(self, s):
        return [(c, c ^ (s * self.rest)) for c in range(self.ctx)]

    def group(self):
        return lax.axis_index("ctx") // self.rest

    def my_bit(self, step, other=0):
        c = lax.axis_index("ctx")
        even = (c >> self.bit(0, step)) & 1
        odd = (c >> self.bit(1, step)) & 1
        return jnp.where((lax.axis_index("dp") + other) % 2 == 0, even, odd)

    def over_rest(self, value, step):
        return lax.ppermute(value, AXES, self.rest_perm(step))

    def over_group(self, value, s):
        return value if s == 0 else lax.ppermute(value, "ctx", self.group_perm(s))

    def gather_rest(self, value):
        blocks = [value]
        for step in range(self.bits):
            came = yield [
                (b, lambda v, step=step: self.over_rest(v, step)) for b in blocks
            ]
            blocks = blocks + came
        return blocks

    def natural(self, pieces, axis=0):
        g = self.group()
        step = 1
        while step < self.groups:
            odd = (g & step) != 0
            pieces = [
                jnp.where(odd, pieces[i ^ step], pieces[i]) for i in range(self.groups)
            ]
            step *= 2
        return jnp.concatenate(pieces, axis=axis)

    def hop(self, step):
        if step < self.bits:
            return lambda v: self.over_rest(v, step)
        return lambda v: self.over_group(v, 1 << (step - self.bits))

    def place_bit(self, step, other=0):
        if step < self.bits:
            return self.my_bit(step, other)
        return (self.group() >> (step - self.bits)) & 1

    def halves(self, value, step):
        half = value.shape[0] // 2
        b = self.place_bit(step)
        return (
            lax.dynamic_slice_in_dim(value, b * half, half, 0),
            lax.dynamic_slice_in_dim(value, (1 - b) * half, half, 0),
        )

    def group_pieces(self, value):
        size = value.shape[0] // self.groups
        return [
            lax.dynamic_slice_in_dim(value, (self.group() ^ s) * size, size, 0)
            for s in range(self.groups)
        ]

    def to_rest(self, value, step):
        return [(value, lambda v: self.over_rest(v, step))]

    def to_groups(self, pieces):
        return [
            (p, lambda v, s=s: self.over_group(v, s)) for s, p in enumerate(pieces) if s
        ]

    def exchange(self, pieces):
        came = yield self.to_groups(pieces)
        return [pieces[0]] + came

    def send_group(self, value, s):
        came = yield [(value, lambda v: self.over_group(v, s))]
        return came[0]

    def scatter_rest(self, parts):
        for step in reversed(range(self.bits)):
            if step < self.bits - 1:
                half = parts.shape[1] // 2
                parts = parts[:, :half], parts[:, half:]
            came = yield self.to_rest(parts[1], step)
            parts = add_low(parts[0], came[0])
        return parts if self.bits else parts[0]

    def reduce_rows(self, value, steps):
        for step in range(steps):
            kept, gone = self.halves(value, step)
            came = yield [(gone, self.hop(step))]
            value = add_low(kept, came[0])
        return value

    def expand_rows(self, value, steps):
        for step in reversed(range(steps)):
            came = yield [(value, self.hop(step))]
            value = jnp.where(
                self.place_bit(step) == 0,
                jnp.concatenate([value, came[0]], axis=0),
                jnp.concatenate([came[0], value], axis=0),
            )
        return value

    def code(self, other):
        steps = self.bits + self.group_bits
        total = 0
        for step in range(steps):
            total = total + (self.place_bit(step, other) << (steps - 1 - step))
        return total

    def sum_blocks(self, pair, stacks):
        steps = self.bits + self.group_bits
        terms = yield from pair.combine(stacks)
        for step in range(steps):
            half = terms[0].shape[0] // 2
            came = yield [(total_low([t[half:] for t in terms]), self.hop(step))]
            terms = [t[:half] for t in terms] + came
        value = total_low(terms)
        for step in reversed(range(steps)):
            came = yield [(value, self.hop(step))]
            halves = [value] + came
            value = jnp.concatenate(halves, axis=0) if step else halves
        return value

    def sum_rows(self, pair, stacks):
        terms = yield from pair.combine(stacks)
        value = yield from self.reduce_rows(total_low(terms), self.bits + self.group_bits)
        return (yield from self.expand_rows(value, self.bits + self.group_bits))

    def sum_heads(self, pair, stacks, columns):
        terms = yield from pair.combine(stacks)
        value = yield from self.reduce_rows(total_low(terms), self.bits)
        rows, groups = value.shape[0], [value]
        for step in range(self.group_bits):
            came = yield [(jnp.concatenate(groups, axis=0), self.hop(self.bits + step))]
            groups = groups + [
                came[0][i * rows : (i + 1) * rows] for i in range(len(groups))
            ]
        value = jnp.concatenate(
            [
                self.natural([p[:, at : at + columns] for p in groups], 1)
                for at in range(0, value.shape[1], columns)
            ],
            axis=1,
        )
        return (yield from self.expand_rows(value, self.bits))


def add_low(a, b):
    return (a.astype(F32) + b.astype(F32)).astype(BF16)


def total_low(terms):
    return functools.reduce(jnp.add, [t.astype(F32) for t in terms]).astype(BF16)


class Chain:
    def __init__(self, name, stages):
        self.name, self.stages, self.came, self.result = name, stages, None, None
        self.stage = 0

    def send(self, moves, values):
        self.stage += 1
        with jax.named_scope(f"{self.name}_{self.stage}"):
            self.came = [move(v) for v, (_, move) in zip(values, moves)]

    def next_moves(self):
        if self.result is not None:
            return []
        try:
            return self.stages.send(self.came)
        except StopIteration as end:
            self.came, self.result = None, end.value
            return []


class Order:
    def __init__(self, token):
        self.token = token

    def __call__(self, land, launch, values=()):
        moves = [c.next_moves() for c in launch]
        waiting = [c for c in land if c not in launch and c.came is not None]
        ended = [c for c in launch if c.result is not None]
        self.token, values, held, done, sent = lax.optimization_barrier(
            (
                self.token,
                values,
                [c.came for c in waiting],
                [c.result for c in ended],
                [[v for v, _ in m] for m in moves],
            )
        )
        for c, came in zip(waiting, held):
            c.came = came
        for c, result in zip(ended, done):
            c.result = result
        for c, m, vs in zip(launch, moves, sent):
            if m:
                c.send(m, vs)
        return values


def finish(*chains):
    while any(c.result is None for c in chains):
        for c in chains:
            m = c.next_moves()
            if m:
                c.send(m, [v for v, _ in m])
    return [c.result for c in chains]


def add_low(a, b):
    return (a.astype(F32) + b.astype(F32)).astype(BF16)


def total_low(terms):
    return functools.reduce(jnp.add, [t.astype(F32) for t in terms]).astype(BF16)


class Pair:
    def __init__(self, dp):
        self.dp = dp
        self.me = lax.axis_index("dp")

    def swap(self, value):
        return lax.ppermute(value, "dp", [(0, 1), (1, 0)])

    def gather(self, weight):
        if self.dp != 2:
            return [lax.all_gather(weight, "dp", axis=0, tiled=True)]
        came = yield [(weight, self.swap)]
        return [weight] + came

    def part(self, value, i, axis):
        if self.dp != 2:
            return value
        half = value.shape[axis] // 2
        at = jnp.where(self.me == i, 0, half)
        return lax.dynamic_slice_in_dim(value, at, half, axis)

    def join(self, parts, axis):
        if len(parts) == 1:
            return parts[0]
        return jnp.where(
            self.me == 0,
            jnp.concatenate(parts, axis),
            jnp.concatenate(parts[::-1], axis),
        )

    def times(self, value, axis, weight, contract):
        return functools.reduce(
            jnp.add,
            [
                contract(self.part(value, i, axis), w)
                for i, w in enumerate(weight)
            ],
        )

    def combine(self, stacks):
        if self.dp == 2:
            came = yield [(stacks[1], self.swap)]
            return [stacks[0]] + came
        return [lax.psum_scatter(stacks[0], "dp", scatter_dimension=0, tiled=True)]


def scaled(rows):
    return lax.rsqrt(jnp.mean(rows * rows, axis=-1, keepdims=True) + EPS)


def norm_back(rows, r, gain, grad):
    lead = gain * grad
    return r * (lead - rows * (r * r) * jnp.mean(lead * rows, axis=-1, keepdims=True))


def gain_grad(gain, *pairs):
    total = sum(jnp.sum(w.astype(F32) * g, axis=1) for w, g in pairs)
    return total / gain.astype(F32)


def on_device(
    dp,
    ctx,
    layer_in,
    out_grad,
    first_gain,
    query_weight,
    key_weight,
    value_weight,
    output_weight,
    second_gain,
    gate_weight,
    up_weight,
    down_weight,
):
    plan, pair = Plan(dp, ctx), Pair(dp)
    _, local, width = layer_in.shape
    ff = gate_weight.shape[1]
    heads, group_width = HEADS // plan.groups, width // plan.groups
    place = jnp.stack([pair.me, plan.group(), plan.code(0), plan.code(1)]).astype(jnp.int32)

    gains_given = jnp.stack([first_gain, second_gain], 1)
    gains_full, w_key, w_value, w_query = finish(
        *[
            Chain("weights", pair.gather(w))
            for w in (gains_given, key_weight, value_weight, query_weight)
        ]
    )
    gains_full = pair.join(gains_full, 0)
    gain_one = gains_full[:, 0].astype(F32)
    x = layer_in.reshape(local, width).astype(F32)
    r1 = scaled(x)
    h1 = (x * r1 * gain_one).astype(BF16)

    def project(w):
        return pair.times(h1, 1, w, lambda a, b: dotg(b, a, 0, 1)).astype(BF16)

    keys, values, query = project(w_key), project(w_value), project(w_query)

    def by_token(value):
        return [value[:, i * local : (i + 1) * local] for i in range(plan.groups)]

    paired = jnp.concatenate(
        [a.reshape(HEADS, HEAD_DIM, local) for a in (keys, values)], axis=1
    ).reshape(2 * width, local)
    order = Order(place)
    kv = Chain("kv", plan.exchange(plan.group_pieces(paired)))
    qs = Chain("qs", plan.exchange(plan.group_pieces(query)))
    later = [
        Chain("weights", pair.gather(w))
        for w in (output_weight, gate_weight, up_weight, down_weight)
    ]
    order([], [kv])
    order([], later[:2])
    order(later[:2], later[2:])
    order(later[2:] + [kv], [qs])
    weights = finish(*later)
    kv = jnp.concatenate(finish(kv)[0], axis=1)
    gather = [
        Chain("keys", plan.gather_rest(kv[2 * HEAD_DIM * h : 2 * HEAD_DIM * (h + 1)]))
        for h in range(heads)
    ]
    spread = [Chain("spread", plan.send_group(h1, i)) for i in range(1, plan.groups)]
    order([], gather[:2])
    for step in range(1, plan.bits):
        order(gather[:1], gather[:1])
    q = jnp.concatenate(finish(qs)[0], axis=1)
    outs = []
    for h in range(heads):
        (sources,) = finish(gather[h])
        coming = gather[h + 1 : h + 2] if plan.bits > 1 else []
        near = spread[:2] if h == 0 else spread[2:] if h == 2 else []
        q, sources, outs = order(
            coming + (spread[h - 1 : h] if h else []), coming + gather[h + 2 : h + 3] + near, (q, sources, outs)
        )
        gather[h].result = sources
        outs = outs + [attend(h, q, sources)]
    o_wide, o_low, lse = zip(*outs)
    sources = [c.result for c in gather]
    mixed = Chain("mixed", plan.exchange(by_token(jnp.concatenate(o_low, axis=0))))
    order([], [mixed])
    order(spread, [mixed])
    mixed = mixed.result
    dy = out_grad.reshape(local, width)
    (layer_out, dy1), do_pieces, made = middle(
        place, dp, ctx, layer_in.reshape(local, width), dy, gains_full[:, 1], mixed, weights, ff
    )
    d_mixed = [
        Chain("d_mixed", plan.send_group(p, s)) for s, p in enumerate(do_pieces) if s
    ]
    order([], d_mixed)
    back = lambda h, do: attend_back(h, q, do, o_wide[h], lse[h], sources[h])

    def sums(stacks):
        return plan.sum_blocks(pair, stacks) if dp == 2 else plan.sum_rows(pair, stacks)

    downs = Chain("downs", sums(made[0]))
    gates = Chain("gates", sums(made[1]))
    ups = Chain("ups", sums(made[2]))
    order([], [downs])
    order([downs], [downs])
    order([], [gates])
    order(d_mixed, [])
    order([], [ups])
    do = jnp.concatenate(do_pieces[:1] + finish(*d_mixed), axis=1)
    do = order([downs, gates], [downs, gates], do)
    dq0, pair0 = back(0, do)
    k0 = Chain("k0", plan.scatter_rest(pair0))
    do, dq0 = order([gates, downs, ups], [ups, gates, downs], (do, dq0))
    dq1, pair1 = back(1, do)
    k1 = Chain("k1", plan.scatter_rest(pair1))
    do, dq1 = order([gates, downs], [gates, downs, k0], (do, dq1))
    dq2, pair2 = back(2, do)
    k2 = Chain("k2", plan.scatter_rest(pair2))
    dq2 = order([k0, gates, downs, ups], [ups, k1, k0, gates, downs], dq2)
    order([k0, downs], [k2, downs])
    order([k1, gates], [k1, gates])
    order([k2, ups], [k2, ups])
    pair0, pair1, pair2 = finish(k0, k1, k2)
    rows = [h1] + finish(*spread)
    third = Chain(
        "third",
        plan.sum_heads(
            pair,
            head_grads(place, dp, (dq0, dq1, dq2), (pair0, pair1, pair2), rows),
            heads * HEAD_DIM,
        ),
    )
    d_all = Chain(
        "d_all",
        plan.exchange(
            by_token(jnp.concatenate([dq0, dq1, dq2, pair0, pair1, pair2], axis=0))
        ),
    )
    order([], [third])
    order([third, gates, downs], [third, gates, downs])
    order([ups], [ups])
    order([third], [third])
    order([gates, downs], [gates, downs])
    order([ups], [ups])
    order([third], [third])
    order([gates], [gates])
    order([ups], [ups])
    order([third], [third])
    order([ups], [ups])
    order([], [d_all])
    order([third], [third])
    order([gates], [])
    order([ups], [ups])
    order([third], [third])
    (gates,) = order([], [], finish(gates))
    order([d_all], [])
    d_all = plan.natural(finish(d_all)[0]).reshape(plan.groups, 3 * heads, HEAD_DIM, local)
    pick = lambda at: jnp.stack([d_all[:, i] for i in at], 1).reshape(width, local)
    d_query = pick(range(heads))
    d_key = pick(range(heads, 3 * heads, 2))
    d_value = pick(range(heads + 1, 3 * heads, 2))
    dh1 = pair.join(
        [
            dotg(d_query, a, 0, 1) + dotg(d_key, b, 0, 1) + dotg(d_value, c, 0, 1)
            for a, b, c in zip(w_query, w_key, w_value)
        ],
        1,
    )
    back_one = norm_back(x, r1, gain_one, dh1)
    in_grad = (back_one + dy1).astype(BF16).reshape(layer_in.shape)

    (third,) = finish(third)
    third = third.astype(F32)
    d_wq, d_wk, d_wv = (third[:, i * width : (i + 1) * width] for i in range(3))
    gain_one_grad = gain_grad(
        first_gain, (query_weight, d_wq), (key_weight, d_wk), (value_weight, d_wv)
    )
    (downs,) = finish(downs)
    if dp == 2:
        (downs,) = ordered(place, *downs, [width])
        d_gate, total = ordered(place, *gates, [ff], (gate_weight,))
    else:
        downs, d_gate = downs.astype(F32), gates.astype(F32)
    early = (in_grad, downs, d_gate, d_wq, d_wk, d_wv, gain_one_grad)
    in_grad, downs, d_gate, d_wq, d_wk, d_wv, gain_one_grad = order([], [], early)
    order([ups], [])
    place = order.token
    (ups,) = finish(ups)
    if dp == 2:
        d_up, d_wo, rest = ordered(place, *ups, [ff, width], (up_weight,))
        gain_two_grad = (total + rest)[:, 0] / second_gain.astype(F32)
    else:
        ups = ups.astype(F32)
        d_up, d_wo = ups[:, :ff], ups[:, ff:]
        gain_two_grad = gain_grad(second_gain, (gate_weight, d_gate), (up_weight, d_up))
    return (
        layer_out.reshape(layer_in.shape),
        in_grad,
        gain_one_grad,
        d_wq,
        d_wk,
        d_wv,
        d_wo,
        gain_two_grad,
        d_gate,
        d_up,
        downs,
    )


def solution(mesh):
    tokens, matrix, vector = P("dp", "ctx", None), P("dp", None), P("dp")
    weights = (vector, matrix, matrix, matrix, matrix, vector, matrix, matrix, matrix)
    return jax.shard_map(
        functools.partial(on_device, mesh.shape["dp"], mesh.shape["ctx"]),
        mesh=mesh,
        in_specs=(tokens, tokens) + weights,
        out_specs=(tokens, tokens) + weights,
        check_vma=False,
    )
```
